512 devices in a mesh: sec: 4 (over x), dom: 128 (over z, y, core).
Axes of the slice: x: 4, y: 8, z: 8, core: 2. Of those that a mesh axis runs over, the one named last changes fastest.
Arguments:
- fields: float32 [4, 64, 131072], P(None, None, ('sec', 'dom')), may hold values from -6 to 6
- source_map: int32 [131072], P(('sec', 'dom')), may hold values from 0 to 255
- new_owner: int32 [32768], P(('sec', 'dom')), may hold values from 0 to 127, as said below
- send_list: int32 [49152], P(('sec', 'dom')), may hold values from -1 to 1535, as said below
- face_slot: int32 [6, 131072], P(None, ('sec', 'dom')), may hold values from -1 to 1631, as said below
Outputs:
- advanced: float32 [4, 64, 131072], P(None, None, ('sec', 'dom'))
The draws below stay inside these ranges and needn't reach their ends.
Inputs may be any that keep to these rules, and one draw needn't show every extreme that they name: source_map names a cell block of the flow device with the same dom index. new_owner names a device of the same section within 2 dom indices; two devices trade as many blocks each way, at most 4; in every section some device trades exactly 4 with each of its 4 nearby devices. send_list holds, for each device, 4 lists of 24 entries for the offsets -2 to -1 and 1 to 2; an entry f * 256 + e names face f of local element e; a list for a device inside the section is full, one for a device outside it is -1. face_slot names for every element face the touching face: the opposite end along the same direction, nodes in the same order, on the same device or in the lists of a device within 2; -1 marks the outer boundary.
All inputs are finite; a program needn't handle non-finite values.
Results may differ from the reference program's by a relative error of at most 0.0003.
Values sent between devices are 32-bit elements; how exact they have to be, the bound alone decides.
No kernel may reach another device: no remote copies, remote signals or barrier semaphores. Data moves between devices by JAX's collectives and lax.ppermute only.
A program may use at most 64 MiB of HBM per device.

```python
import jax
import jax.numpy as jnp
import numpy as np
from jax import lax

ELEMENTS = 256
BLOCK_SIZE = 4
MOVE_CAP = 4
SPREAD = 2
CHAIN_LEN = 8
CHAIN_SENDS = 4
BLOCKS = 64
FACE_CAP = 24
ALL_ELEMENTS = 131072
N_SEC = 4
N_DOM = 128


def owner_section(key):
    pair_key, star_key, perm_key = jax.random.split(key, 3)
    trades = jax.random.randint(pair_key, (N_DOM, SPREAD), 0, MOVE_CAP + 1)
    device = jnp.arange(N_DOM)
    reach = jnp.arange(1, SPREAD + 1)
    inside = device[:, None] + reach[None, :] < N_DOM
    star = jax.random.randint(star_key, (), SPREAD, N_DOM - SPREAD)
    forced = (device[:, None] == star) | (device[:, None] + reach[None, :] == star)
    trades = jnp.where(forced, MOVE_CAP, trades)
    trades = jnp.where(inside, trades, 0)
    downward = jnp.stack([jnp.where(device - offset_value >= 0, trades[jnp.clip(device - offset_value, 0), offset_value - 1], 0) for offset_value in range(SPREAD, 0, -1)], axis=1)
    counts = jnp.concatenate([downward, trades], axis=1)
    offsets = jnp.concatenate([jnp.arange(-SPREAD, 0), jnp.arange(1, SPREAD + 1)])
    running = jnp.cumsum(counts, axis=1)
    position = jnp.arange(BLOCKS)
    slot_number = jnp.sum(position[None, :, None] >= running[:, None, :], axis=2)
    target = jnp.where(slot_number < 2 * SPREAD, device[:, None] + offsets[jnp.clip(slot_number, 0, 2 * SPREAD - 1)], device[:, None])
    shuffles = jax.vmap(lambda subkey: jax.random.permutation(subkey, BLOCKS))(jax.random.split(perm_key, N_DOM))
    return jnp.take_along_axis(target, shuffles, axis=1).reshape(-1).astype(jnp.int32)


def draw_new_owner(key, part):
    sections = jax.vmap(lambda number: owner_section(jax.random.fold_in(key, number)))(jnp.arange(N_SEC))
    return sections.reshape(-1).astype(jnp.int32)


def slot_of(offset_value):
    return jnp.where(offset_value < 0, offset_value + SPREAD, offset_value + SPREAD - 1)


def face_section(key):
    offsets = jnp.concatenate([jnp.arange(-SPREAD, 0), jnp.arange(1, SPREAD + 1)])
    chains = ELEMENTS // CHAIN_LEN
    device = jnp.arange(N_DOM)
    rows = device[:, None]
    dump = 2 * SPREAD * FACE_CAP
    slots = jnp.full((N_DOM, 6, ELEMENTS), -1, jnp.int32)
    sends = jnp.full((N_DOM, dump + 1), -1, jnp.int32)
    for direction in range(3):
        axis_key = jax.random.fold_in(key, direction)
        shuffles = jax.vmap(lambda subkey: jax.random.permutation(subkey, ELEMENTS))(jax.random.split(jax.random.fold_in(axis_key, 1), N_DOM))
        base = jnp.concatenate([jnp.zeros(chains - 2 * SPREAD * CHAIN_SENDS, jnp.int32), jnp.repeat(offsets, CHAIN_SENDS).astype(jnp.int32)])
        chain_off = jax.random.permutation(jax.random.fold_in(axis_key, 2), base)
        links = shuffles.reshape(N_DOM, chains, CHAIN_LEN)
        lower = 2 * direction
        upper = 2 * direction + 1
        left = links[:, :, :-1].reshape(N_DOM, -1)
        right = links[:, :, 1:].reshape(N_DOM, -1)
        slots = slots.at[rows, upper, left].set(lower * ELEMENTS + right)
        slots = slots.at[rows, lower, right].set(upper * ELEMENTS + left)
        ends = links[:, :, -1]
        starts = links[:, :, 0]
        match = (chain_off[:, None] == offsets[None, :]).astype(jnp.int32)
        ranking = jnp.sum((jnp.cumsum(match, axis=0) - 1) * match, axis=1)
        own_slot = slot_of(chain_off)
        back_slot = slot_of(-chain_off)
        target = device[:, None] + chain_off[None, :]
        source = device[:, None] - chain_off[None, :]
        upward_ok = (target >= 0) & (target < N_DOM)
        downward_ok = (source >= 0) & (source < N_DOM)
        local = (chain_off == 0)[None, :]
        remote_upper = 6 * ELEMENTS + own_slot * FACE_CAP + direction * 2 * CHAIN_SENDS + CHAIN_SENDS + ranking
        remote_lower = 6 * ELEMENTS + back_slot * FACE_CAP + direction * 2 * CHAIN_SENDS + ranking
        upper_value = jnp.where(local, lower * ELEMENTS + starts, jnp.where(upward_ok, remote_upper[None, :], -1))
        lower_value = jnp.where(local, upper * ELEMENTS + ends, jnp.where(downward_ok, remote_lower[None, :], -1))
        slots = slots.at[rows, upper, ends].set(upper_value.astype(jnp.int32))
        slots = slots.at[rows, lower, starts].set(lower_value.astype(jnp.int32))
        end_place = jnp.where(local | ~upward_ok, dump, (own_slot * FACE_CAP + direction * 2 * CHAIN_SENDS + ranking)[None, :])
        sends = sends.at[rows, end_place].set(upper * ELEMENTS + ends)
        start_place = jnp.where(local | ~downward_ok, dump, (back_slot * FACE_CAP + direction * 2 * CHAIN_SENDS + CHAIN_SENDS + ranking)[None, :])
        sends = sends.at[rows, start_place].set(lower * ELEMENTS + starts)
    return (sends[:, :dump], slots)


def face_lists(key):
    return jax.vmap(lambda number: face_section(jax.random.fold_in(key, number)))(jnp.arange(N_SEC))


def draw_send_list(key, part):
    sends, slots = face_lists(key)
    return sends.reshape(-1).astype(jnp.int32)


def draw_face_slot(key, part):
    sends, slots = face_lists(key)
    return jnp.transpose(slots, (2, 0, 1, 3)).reshape(6, -1).astype(jnp.int32)


def touch_ends(values, stream_key, low, largest):
    dims = values.shape
    index_at = [jax.random.randint(jax.random.fold_in(stream_key, axis), (), 0, dims[axis]) for axis in range(len(dims))]
    values = values.at[tuple(index_at)].set(low)
    longest = dims.index(max(dims))
    index_at[longest] = (index_at[longest] + 1) % dims[longest]
    return values.at[tuple(index_at)].set(largest)


def levels(key, dims, shards, least, high):
    def one(dim, blocks):
        steps = jax.random.uniform(jax.random.fold_in(jax.random.fold_in(key, 6), dim), (blocks,), jnp.float32, least / len(shards), high / len(shards))
        return jnp.repeat(jnp.exp(steps), dims[dim] // blocks).reshape((-1,) + (1,) * (len(dims) - dim - 1))

    loudness = one(*shards[0])
    for cut in shards[1:]:
        loudness = loudness * one(*cut)
    return loudness


def normal_values(stream_key, dims, deviation, limit, cuts=(), held_as=jnp.bfloat16):
    gain = levels(stream_key, dims, cuts, -0.22, 0.18) if cuts else 1.0
    drawn = jax.random.normal(stream_key, dims, jnp.float32) * deviation * gain
    return jnp.minimum(jnp.maximum(drawn, -limit), limit).astype(held_as)


def setup_inputs(seed: int = 0) -> dict:
    key_of = jax.random.split(jax.random.key(seed), 6)
    return {
        "fields": normal_values(key_of[0], (4, 64, ALL_ELEMENTS), 1.0, 6.0, ((2, 512),), jnp.float32),
        "source_map": touch_ends(jax.random.randint(key_of[1], (ALL_ELEMENTS,), 0, ELEMENTS), jax.random.fold_in(key_of[1], 1), 0, ELEMENTS - 1).astype(jnp.int32),
        "new_owner": draw_new_owner(jax.random.fold_in(key_of[5], 71), 0),
        "send_list": draw_send_list(jax.random.fold_in(key_of[5], 71), 0),
        "face_slot": draw_face_slot(jax.random.fold_in(key_of[5], 71), 0),
    }


CELL_DIFFERENCE = [[-1.0, 1.0, 0.0, 0.0], [-0.5, 0.0, 0.5, 0.0], [0.0, -0.5, 0.0, 0.5], [0.0, 0.0, -1.0, 1.0]]
SEGMENT_CARRY = [0.0, -567301805773.0 / 1357537059087.0, -2404267990393.0 / 2016746695238.0, -3550918686646.0 / 2091501179385.0, -1275806237668.0 / 842570457699.0]
SEGMENT_WEIGHTS = [1432997174477.0 / 9575080441755.0, 5161836677717.0 / 13612068292357.0, 1720146321549.0 / 2090206949498.0, 3134564353537.0 / 4481467310338.0, 2277821191437.0 / 14882151754819.0]
TIME_STEP = 0.12
END_LIFT = 6.0

def node_derivative():
    points = np.array([-1.0, -1.0 / np.sqrt(5.0), 1.0 / np.sqrt(5.0), 1.0])
    products = np.array([np.prod([points[row] - points[col] for col in range(4) if col != row]) for row in range(4)])
    matrix = np.zeros((4, 4))
    for row in range(4):
        for col in range(4):
            if row != col:
                matrix[row, col] = products[row] / (products[col] * (points[row] - points[col]))
        matrix[row, row] = -np.sum(matrix[row])
    return matrix

def derivative_along(matrix, field, direction):
    forms = ['mi,ijke->mjke', 'mj,ijke->imke', 'mk,ijke->ijme']
    return jnp.einsum(forms[direction], matrix, field, precision=lax.Precision.HIGHEST)

def lamb_vector(cells):
    cube = cells.reshape(4, 4, 4, 4, -1)
    matrix = jnp.asarray(CELL_DIFFERENCE, cells.dtype)

    def slope(component, direction):
        return derivative_along(matrix, cube[component], direction)
    spin_x = slope(2, 1) - slope(1, 2)
    spin_y = slope(0, 2) - slope(2, 0)
    spin_z = slope(1, 0) - slope(0, 1)
    lamb_x = spin_y * cube[2] - spin_z * cube[1]
    lamb_y = spin_z * cube[0] - spin_x * cube[2]
    lamb_z = spin_x * cube[1] - spin_y * cube[0]
    return (cube[3] * jnp.stack([lamb_x, lamb_y, lamb_z])).reshape(3, 64, -1)

def face_traces(state_now):
    cube = state_now.reshape(4, 4, 4, 4, -1)
    faces = [cube[:, 0], cube[:, 3], cube[:, :, 0], cube[:, :, 3], cube[:, :, :, 0], cube[:, :, :, 3]]
    return jnp.stack([piece.reshape(4, 16, -1) for piece in faces], axis=2).reshape(4, 16, -1)

def exterior(traces, received, slots_here):
    lookup = jnp.concatenate([traces, received], axis=2)
    flat_slots = slots_here.reshape(-1)
    outside = jnp.take(lookup, jnp.clip(flat_slots, 0), axis=2) * (flat_slots >= 0)
    return outside.reshape(4, 16, 6, -1)

def tendency(state_now, traces, outside, forcing):
    elements = state_now.shape[2]
    cube = state_now.reshape(4, 4, 4, 4, elements)
    matrix = jnp.asarray(node_derivative(), state_now.dtype)
    divergence = derivative_along(matrix, cube[1], 0) + derivative_along(matrix, cube[2], 1) + derivative_along(matrix, cube[3], 2)
    force_cube = forcing.reshape(3, 4, 4, 4, elements)
    pieces = [-divergence] + [force_cube[direction] - derivative_along(matrix, cube[0], direction) for direction in range(3)]
    result = jnp.stack(pieces)
    inside = traces.reshape(4, 16, 6, elements)
    for direction in range(3):
        for face_side in range(2):
            face_index = 2 * direction + face_side
            normal_sign = 2.0 * face_side - 1.0
            jump_value = outside[:, :, face_index] - inside[:, :, face_index]
            correction = 0.5 * jump_value
            correction = correction.at[0].add(-0.5 * normal_sign * jump_value[1 + direction])
            correction = correction.at[1 + direction].add(-0.5 * normal_sign * jump_value[0])
            lifted = (END_LIFT * correction).reshape(4, 4, 4, elements)
            where_index = (slice(None),) * (direction + 1) + (3 * face_side,)
            result = result.at[where_index].add(lifted)
    return result.reshape(4, 64, elements)

def reference(fields, source_map, new_owner, send_list, face_slot):
    sections = N_SEC
    domains = N_DOM
    elements = ELEMENTS
    blocks = BLOCKS
    devices = sections * domains
    slot_total = 2 * SPREAD * FACE_CAP
    lamb_source = lamb_vector(fields[:, :, :domains * elements])
    section_maps = source_map.reshape(sections, domains, elements)
    flat_source = (jnp.arange(domains, dtype=jnp.int32)[None, :, None] * elements + section_maps).reshape(-1).astype(jnp.int32)
    forcing_cols = jnp.take(lamb_source, flat_source, axis=2)
    packed = jnp.concatenate([fields, forcing_cols], axis=0)
    owners = new_owner.reshape(sections, domains * blocks)
    block_ids = jnp.arange(domains * blocks, dtype=jnp.int32)
    source_dom = block_ids // blocks
    local_block = block_ids % blocks
    step_away = source_dom[None, :] - owners
    rank_group = jnp.where(step_away == 0, 0, step_away + SPREAD + 1)
    sort_key = owners * ((2 * SPREAD + 2) * blocks) + rank_group * blocks + local_block[None, :]
    new_order = jnp.argsort(sort_key, axis=1).astype(jnp.int32)
    element_src = (new_order[:, :, None] * BLOCK_SIZE + jnp.arange(BLOCK_SIZE, dtype=jnp.int32)[None, None, :]).reshape(sections, -1)
    element_src = element_src + (jnp.arange(sections, dtype=jnp.int32) * (domains * elements))[:, None]
    placed = jnp.take(packed, element_src.reshape(-1).astype(jnp.int32), axis=2)
    state_now = placed[:4]
    forcing = placed[4:]
    carry_rate = jnp.zeros_like(state_now)
    send_rows = send_list.reshape(devices, slot_total)
    offsets = [value for value in range(-SPREAD, SPREAD + 1) if value != 0]
    device_ids = jnp.arange(devices, dtype=jnp.int32)
    for segment_index in range(5):

        def gather_sent(item):
            device_id, send_row = item
            local = lax.dynamic_slice_in_dim(state_now, device_id * elements, elements, 2)
            traces = face_traces(local)
            return jnp.take(traces, jnp.clip(send_row, 0), axis=2) * (send_row >= 0)
        sent = lax.map(gather_sent, (device_ids, send_rows))
        sent = sent.reshape(sections, domains, 4, 16, 2 * SPREAD, FACE_CAP)
        incoming = []
        for slot_index, offset_value in enumerate(offsets):
            piece = sent[:, :, :, :, 2 * SPREAD - 1 - slot_index]
            if offset_value > 0:
                piece = jnp.concatenate([piece[:, offset_value:], jnp.zeros_like(piece[:, :offset_value])], axis=1)
            else:
                back = -offset_value
                piece = jnp.concatenate([jnp.zeros_like(piece[:, :back]), piece[:, :-back]], axis=1)
            incoming.append(piece)
        received = jnp.stack(incoming, axis=4).reshape(devices, 4, 16, slot_total)

        def device_rate(item):
            device_id, recv_block = item
            local = lax.dynamic_slice_in_dim(state_now, device_id * elements, elements, 2)
            local_force = lax.dynamic_slice_in_dim(forcing, device_id * elements, elements, 2)
            slots_here = lax.dynamic_slice_in_dim(face_slot, device_id * elements, elements, 1)
            traces = face_traces(local)
            outside = exterior(traces, recv_block, slots_here)
            rate_here = tendency(local, traces, outside, local_force)
            return jnp.where(device_id >= domains, rate_here, jnp.zeros_like(rate_here))
        rates = lax.map(device_rate, (device_ids, received))
        rates = jnp.transpose(rates, (1, 2, 0, 3)).reshape(4, 64, -1)
        carry_rate = SEGMENT_CARRY[segment_index] * carry_rate + TIME_STEP * rates
        state_now = state_now + SEGMENT_WEIGHTS[segment_index] * carry_rate
    return state_now
```

```python
import functools

import jax
import jax.numpy as jnp
import numpy as np
from jax import lax
from jax.experimental import pallas as pl
from jax.experimental.pallas import tpu as pltpu
from jax.sharding import PartitionSpec as P

SPREAD = 2
FACE_CAP = 24
MOVED = 16
OFFSETS = (-2, -1, 1, 2)
LANES = 128
ELEMENTS = 256
ROWS = 256
TRACE_ROWS = 48
LIFT = 3.0
TIME_STEP = 0.12
SEGMENT_CARRY = [
    0.0,
    -567301805773.0 / 1357537059087.0,
    -2404267990393.0 / 2016746695238.0,
    -3550918686646.0 / 2091501179385.0,
    -1275806237668.0 / 842570457699.0,
]
SEGMENT_WEIGHTS = [
    1432997174477.0 / 9575080441755.0,
    5161836677717.0 / 13612068292357.0,
    1720146321549.0 / 2090206949498.0,
    3134564353537.0 / 4481467310338.0,
    2277821191437.0 / 14882151754819.0,
]
CELL_DIFFERENCE = np.array(
    [[-1.0, 1.0, 0.0, 0.0], [-0.5, 0.0, 0.5, 0.0], [0.0, -0.5, 0.0, 0.5], [0.0, 0.0, -1.0, 1.0]]
)
BF = jnp.bfloat16
F32 = jnp.float32


def node_derivative():
    points = np.array([-1.0, -1.0 / np.sqrt(5.0), 1.0 / np.sqrt(5.0), 1.0])
    products = np.array(
        [np.prod([points[row] - points[col] for col in range(4) if col != row]) for row in range(4)]
    )
    matrix = np.zeros((4, 4))
    for row in range(4):
        for col in range(4):
            if row != col:
                matrix[row, col] = products[row] / (products[col] * (points[row] - points[col]))
        matrix[row, row] = -np.sum(matrix[row])
    return matrix


def along(matrix, direction):
    eye = np.eye(4)
    parts = [eye, eye, eye]
    parts[direction] = matrix
    return np.kron(np.kron(parts[0], parts[1]), parts[2])


def face_nodes(face):
    direction, side = divmod(face, 2)
    index = np.arange(64).reshape(4, 4, 4)
    return np.take(index, 3 * side, axis=direction).reshape(-1)


def spin_matrix():
    slopes = [along(CELL_DIFFERENCE, direction) for direction in range(3)]
    zero = np.zeros((64, 64))
    return np.block(
        [
            [zero, -slopes[2], slopes[1]],
            [slopes[2], zero, -slopes[0]],
            [-slopes[1], slopes[0], zero],
        ]
    )


def interior_matrix():
    derivative = node_derivative()
    total = np.zeros((256, 256))
    for a in range(3):
        d = along(derivative, a)
        total[0:64, 64 * (a + 1) : 64 * (a + 2)] -= d
        total[64 * (a + 1) : 64 * (a + 2), 0:64] -= d
    for face in range(6):
        a, side = divmod(face, 2)
        sign = 2.0 * side - 1.0
        nodes = face_nodes(face)
        va = 64 * (a + 1) + nodes
        total[nodes, nodes] -= LIFT
        total[nodes, va] += LIFT * sign
        total[va, va] -= LIFT
        total[va, nodes] += LIFT * sign
        for b in range(3):
            if b != a:
                vb = 64 * (b + 1) + nodes
                total[vb, vb] -= LIFT
    return total


def trace_matrix():
    total = np.zeros((6 * TRACE_ROWS, 256))
    for face in range(6):
        a, side = divmod(face, 2)
        sign = 2.0 * side - 1.0
        nodes = face_nodes(face)
        rows = TRACE_ROWS * face + np.arange(16)
        total[rows, nodes] = 1.0
        total[rows, 64 * (a + 1) + nodes] = sign
        for number, b in enumerate([b for b in range(3) if b != a]):
            total[rows + 16 * (number + 1), 64 * (b + 1) + nodes] = 1.0
    return total


def lift_matrix():
    total = np.zeros((256, 6 * TRACE_ROWS))
    for face in range(6):
        a, side = divmod(face, 2)
        sign = 2.0 * side - 1.0
        nodes = face_nodes(face)
        cols = TRACE_ROWS * face + np.arange(16)
        total[nodes, cols] = 1.0
        total[64 * (a + 1) + nodes, cols] = -sign
        for number, b in enumerate([b for b in range(3) if b != a]):
            total[64 * (b + 1) + nodes, cols + 16 * (number + 1)] = 1.0
    return total


def two_terms(matrix):
    high = matrix.astype(np.float32).astype(BF)
    low = (matrix - high.astype(np.float64)).astype(np.float32).astype(BF)
    return high, low


def mm(a, b):
    return lax.dot_general(a, b, (((1,), (0,)), ((), ())), preferred_element_type=F32)


def mm_nt(a, b):
    return lax.dot_general(a, b, (((1,), (1,)), ((), ())), preferred_element_type=F32)


def split(x):
    high = x.astype(BF)
    return high, (x - high.astype(F32)).astype(BF)


def one_hot(mask):
    return jnp.where(mask, 1.0, 0.0).astype(BF)


def lane_iota(shape):
    return lax.broadcasted_iota(jnp.int32, shape, 1)


def row_iota(shape):
    return lax.broadcasted_iota(jnp.int32, shape, 0)


def select_columns(x, chosen_nt):
    high, low = split(x)
    return mm_nt(high, chosen_nt) + mm_nt(low, chosen_nt)


def pack_pieces(sent, outs):
    lane = lane_iota((16, LANES))
    for slot in range(4):
        total = jnp.zeros((16, LANES), F32)
        for chunk in range(3):
            move = (FACE_CAP * (chunk - slot)) % LANES
            part = sent[16 * chunk : 16 * chunk + 16]
            if move:
                part = pltpu.roll(part, move, 1)
            inside = (lane >= FACE_CAP * chunk) & (lane < FACE_CAP * (chunk + 1))
            total = jnp.where(inside, part, total)
        outs[slot][...] = total


def unpack_pieces(pieces):
    lane = lane_iota((16, LANES))
    chunks = []
    for chunk in range(3):
        total = jnp.zeros((16, LANES), F32)
        for slot in range(4):
            move = (FACE_CAP * (slot - chunk)) % LANES
            part = pieces[slot][...]
            if move:
                part = pltpu.roll(part, move, 1)
            inside = (lane >= FACE_CAP * slot) & (lane < FACE_CAP * (slot + 1))
            total = jnp.where(inside, part, total)
        chunks.append(total)
    return jnp.concatenate(chunks, axis=0)


def send_traces(state, pick, kinds, trace, outs):
    high, low = split(state)
    chosen = jnp.concatenate([mm(high, pick).astype(BF), mm(low, pick).astype(BF)], axis=1)
    shown = mm(trace, chosen)
    shown = shown[:, :LANES] + shown[:, LANES:]
    sent = jnp.zeros((TRACE_ROWS, LANES), F32)
    for face in range(6):
        part = shown[TRACE_ROWS * face : TRACE_ROWS * (face + 1)]
        sent = sent + jnp.where(kinds[face : face + 1] > 0, part, 0.0)
    pack_pieces(sent, outs)


def received_rates(pieces, kinds, lift, place):
    got = unpack_pieces(pieces)
    masked = jnp.concatenate(
        [jnp.where(kinds[face : face + 1] > 0, got, 0.0) for face in range(6)], axis=0
    )
    high, low = split(masked)
    spread = mm(lift, jnp.concatenate([high, low], axis=1)).astype(BF)
    return mm(spread, place)


def lamb_kernel(cells, spin, *outs):
    u = cells[0:192]
    high, low = split(u)
    omega = mm(spin[...], high) + mm(spin[...], low)
    w = [omega[64 * a : 64 * (a + 1)] for a in range(3)]
    v = [u[64 * a : 64 * (a + 1)] for a in range(3)]
    rho = cells[192:256]
    pieces = [
        rho * (w[1] * v[2] - w[2] * v[1]),
        rho * (w[2] * v[0] - w[0] * v[2]),
        rho * (w[0] * v[1] - w[1] * v[0]),
    ]
    lamb = jnp.concatenate(pieces, axis=0)
    outs[0][...] = lamb[:96]
    outs[1][...] = lamb[96:]


def depart_kernel(cells, owner, out0, out1, out2, out3, keep_out, select_out, place_out):
    me = lax.axis_index("dom")
    away = (owner[...] - me).astype(F32)
    away = jnp.broadcast_to(away, (8, 64))
    away = jnp.clip(away, -8.0, 8.0).astype(BF)
    spread = one_hot((lane_iota((64, 256)) >> 2) == row_iota((64, 256)))
    away = mm(away, spread)
    group = row_iota((8, 256))
    wanted = jnp.where(group < 2, group - 2, group - 1)
    wanted = jnp.where(group == 4, 0, wanted).astype(F32)
    member = (away == wanted) & (group < 5)
    member_f = jnp.where(member, 1.0, 0.0)
    before = one_hot(row_iota((256, 256)) < lane_iota((256, 256)))
    rank = mm(member_f.astype(BF), before)
    count = jnp.sum(member_f, axis=1, keepdims=True)
    lane = lane_iota((8, 256))
    groupf = group.astype(F32)
    target = jnp.sum(
        jnp.where(member & (group < 4), rank + 16.0 * groupf + 1.0, 0.0), axis=0, keepdims=True
    ) - 1.0
    kept = jnp.sum(jnp.where(member & (group == 4), rank + 1.0, 0.0), axis=0, keepdims=True) - 1.0
    select = one_hot(target == row_iota((64, 256)).astype(F32))
    high, low = split(cells[...])
    sent = mm_nt(select, high) + mm_nt(select, low)
    for slot, out in enumerate((out0, out1, out2, out3)):
        out[...] = sent[16 * slot : 16 * slot + 16]
    select_out[...] = select
    keep_out[...] = one_hot(kept == row_iota((256, 256)).astype(F32))
    start = count[4:5]
    ahead = lane_iota((16, 256)).astype(F32)
    number = row_iota((16, 256)).astype(F32)
    for slot in range(4):
        amount = count[slot : slot + 1]
        place_out[16 * slot : 16 * slot + 16, :] = one_hot(
            (ahead - start == number) & (number < amount)
        )
        start = start + amount


def tables_kernel(
    cells, keep, select, source, sends, slots,
    kept_out, source_keep_out, source_select_out, local_out, place_out, kinds_out, pick_out,
    send_kinds_out,
):
    kept_out[...] = select_columns(cells[...], keep[...])
    names = (source[...] + 1).astype(F32)
    moved = mm_nt(jnp.broadcast_to(names, (8, 256)).astype(BF), keep[...])
    rows = row_iota((256, 256)).astype(F32) + 1.0
    source_keep_out[...] = one_hot(moved[0:1] == rows)
    chosen = jnp.sum(select[...].astype(F32) * names, axis=1, keepdims=True)
    source_select_out[...] = one_hot(chosen == lane_iota((64, 256)).astype(F32) + 1.0)
    row = row_iota((256, 256))
    entry = row_iota((LANES, 256)) + 6 * ELEMENTS
    ones = jnp.ones((8, 256), BF)
    place = jnp.zeros((LANES, 256), F32)
    kinds_out[...] = jnp.zeros_like(kinds_out)
    for face in range(6):
        where = slots[face : face + 1]
        local_out[face] = one_hot(where - ELEMENTS * (face ^ 1) == row)
        hit = jnp.where(where == entry, 1.0, 0.0)
        place = place + hit
        kinds_out[face : face + 1] = mm_nt(ones, hit.astype(BF))[0:1]
    place_out[0:LANES] = place.astype(BF)
    place_out[LANES : 2 * LANES] = place.astype(BF)
    names = sends[...]
    pick_out[...] = one_hot((names & 255) + jnp.where(names < 0, -512, 0) == row_iota((256, LANES)))
    send_kinds_out[...] = jnp.where((names >> 8) == row_iota((8, LANES)), 1.0, 0.0)


def arrive_kernel(
    in0, in1, in2, in3, kept, place, pick, send_kinds, trace, state_out, out0, out1, out2, out3
):
    got = jnp.concatenate([in0[...], in1[...], in2[...], in3[...]], axis=0)
    high, low = split(jnp.transpose(got))
    state = kept[...] + (mm(high, place[...]) + mm(low, place[...]))
    state_out[...] = state
    send_traces(state, pick[...], send_kinds[...], trace[...], (out0, out1, out2, out3))


def force_kernel(*refs):
    parts, source_select, source_keep = refs[:6], refs[6], refs[7]
    out0, out1, out2, out3, kept_out = refs[8:]
    upper = parts[0][...] + parts[1][...] + parts[2][...]
    lower = parts[3][...] + parts[4][...] + parts[5][...]
    lamb = jnp.concatenate([upper, lower], axis=0)
    high, low = split(lamb)
    sent = mm_nt(source_select[...], high) + mm_nt(source_select[...], low)
    for slot, out in enumerate((out0, out1, out2, out3)):
        out[...] = sent[16 * slot : 16 * slot + 16]
    kept_out[...] = mm(high, source_keep[...]) + mm(low, source_keep[...])


def local_rates(state, local, interior, trace, lift):
    high, low = split(state)
    rates = mm(interior, jnp.concatenate([high, low, high], axis=0))
    shown = mm(trace, high) + mm(trace, low)
    shown_high, shown_low = split(shown)
    outside_high, outside_low = [], []
    for face in range(6):
        other = TRACE_ROWS * (face ^ 1)
        stacked = jnp.concatenate(
            [shown_high[other : other + TRACE_ROWS], shown_low[other : other + TRACE_ROWS]], axis=0
        )
        found = mm(stacked, local[face]).astype(BF)
        outside_high.append(found[:TRACE_ROWS])
        outside_low.append(found[TRACE_ROWS:])
    outside = jnp.concatenate(outside_high + outside_low, axis=0)
    return rates + LIFT * mm(lift, outside)


def inner_kernel(segment, state, local, interior, trace, lift, *rest):
    rates = local_rates(state[...], local, interior[...], trace[...], lift[...])
    if segment == 0:
        (carry_out,) = rest
        carry_out[...] = TIME_STEP * rates
        return
    carry, force, carry_out = rest
    own = SEGMENT_CARRY[segment] * carry[...] + TIME_STEP * rates
    carry_out[0:64] = own[0:64]
    carry_out[64:256] = own[64:256] + TIME_STEP * force[...]


def outer_kernel(segment, *refs):
    pieces, refs = refs[:4], refs[4:]
    (state, carry, kinds, place, lift), refs = refs[:5], refs[5:]
    acoustic = lax.axis_index("sec") > 0
    weight = jnp.where(acoustic, F32(SEGMENT_WEIGHTS[segment]), F32(0.0))
    rates = received_rates(pieces, kinds[...], lift[...], place[...])
    carry_now = carry[...] + (LIFT * TIME_STEP) * rates
    if segment == 0:
        (in0, in1, in2, in3, kept_force, arrive), refs = refs[:6], refs[6:]
        got = jnp.concatenate([in0[...], in1[...], in2[...], in3[...]], axis=0)
        high, low = split(jnp.transpose(got))
        force = kept_force[...] + (mm(high, arrive[...]) + mm(low, arrive[...]))
        carry_now = jnp.concatenate(
            [carry_now[0:64], carry_now[64:256] + TIME_STEP * force], axis=0
        )
    state_now = state[...] + weight * carry_now
    if segment == 4:
        refs[0][...] = state_now
        return
    (pick, send_kinds, trace), refs = refs[:3], refs[3:]
    refs[0][...] = state_now
    refs[1][...] = carry_now
    send_traces(state_now, pick[...], send_kinds[...], trace[...], refs[2:6])
    if segment == 0:
        refs[6][...] = force


def call(kernel, outs, *args, flops=1 << 20):
    vmem = pl.BlockSpec(memory_space=pltpu.VMEM)
    size = sum(int(np.prod(a.shape)) * a.dtype.itemsize for a in (*args, *outs))
    return pl.pallas_call(
        kernel,
        out_shape=list(outs),
        in_specs=[vmem] * len(args),
        out_specs=[vmem] * len(outs),
        compiler_params=pltpu.CompilerParams(vmem_limit_bytes=24 << 20),
        cost_estimate=pl.CostEstimate(flops=flops, bytes_accessed=size, transcendentals=0),
    )(*args)


def arr(*shape, dtype=F32):
    return jax.ShapeDtypeStruct(shape, dtype)


def shift(value, steps):
    count = lax.axis_size("dom")
    first, last = max(0, -steps), min(count, count - steps)
    return lax.ppermute(value, "dom", [(source, source + steps) for source in range(first, last)])


def exchange(pieces):
    arrived = [None] * 4
    for slot, offset in enumerate(OFFSETS):
        arrived[3 - slot] = shift(pieces[slot], offset)
    return arrived


def spread_from_flow(upper, lower):
    def hop(value, source, target):
        return lax.ppermute(value, "sec", [(source, target)])

    upper_1, lower_3 = hop(upper, 0, 1), hop(lower, 0, 3)
    lower_1, upper_3 = hop(lower, 0, 1), hop(upper, 0, 3)
    upper_2, lower_2 = hop(upper_1, 1, 2), hop(lower_3, 3, 2)
    return upper_1, upper_2, upper_3, lower_1, lower_2, lower_3


def local(fields, source_map, new_owner, send_list, face_slot):
    cells = fields.reshape(ROWS, ELEMENTS)
    spin = jnp.asarray(spin_matrix().astype(BF))
    high, low = two_terms(interior_matrix())
    interior = jnp.asarray(np.concatenate([high, high, low], axis=1))
    trace = jnp.asarray(trace_matrix().astype(BF))
    lift_np = lift_matrix().astype(BF)
    lift = jnp.asarray(lift_np)
    lift_two = jnp.asarray(np.concatenate([lift_np, lift_np], axis=1))
    piece = arr(16, LANES)

    halves = call(lamb_kernel, [arr(96, 256)] * 2, cells, spin)
    lamb_parts = spread_from_flow(*halves)
    *leaving, keep, select, arrive = call(
        depart_kernel,
        [arr(MOVED, 256)] * 4 + [arr(256, 256, dtype=BF), arr(64, 256, dtype=BF), arr(64, 256, dtype=BF)],
        cells,
        new_owner.reshape(1, 64),
    )
    moved = exchange(leaving)
    sends = jnp.pad(send_list, (0, LANES - 4 * FACE_CAP), constant_values=-1).reshape(1, LANES)
    kept, source_keep, source_select, near, place, kinds, pick, send_kinds = call(
        tables_kernel,
        [
            arr(256, 256),
            arr(256, 256, dtype=BF),
            arr(64, 256, dtype=BF),
            arr(6, 256, 256, dtype=BF),
            arr(256, 256, dtype=BF),
            arr(8, LANES),
            arr(256, LANES, dtype=BF),
            arr(8, LANES),
        ],
        cells,
        keep,
        select,
        source_map.reshape(1, 256),
        sends,
        face_slot,
    )
    state, *pieces = call(
        arrive_kernel, [arr(256, 256)] + [piece] * 4, *moved, kept, arrive, pick, send_kinds, trace
    )
    pieces = exchange(pieces)
    *leaving, kept_force = call(
        force_kernel,
        [arr(MOVED, 192)] * 4 + [arr(192, 256)],
        *lamb_parts,
        source_select,
        source_keep,
    )
    moved_force = exchange(leaving)
    carry = force = None
    for segment in range(5):
        extra = [] if segment == 0 else [carry, force]
        (carry,) = call(
            functools.partial(inner_kernel, segment),
            [arr(256, 256)],
            state, near, interior, trace, lift_two, *extra,
        )
        args = [*pieces, state, carry, kinds, place, lift]
        outs = [arr(256, 256)]
        if segment == 0:
            args += [*moved_force, kept_force, arrive]
        if segment < 4:
            args += [pick, send_kinds, trace]
            outs += [arr(256, 256)] + [piece] * 4
        if segment == 0:
            outs += [arr(192, 256)]
        results = call(functools.partial(outer_kernel, segment), outs, *args)
        state = results[0]
        if segment < 4:
            carry = results[1]
            pieces = exchange(results[2:6])
        if segment == 0:
            force = results[6]
    return state.reshape(4, 64, ELEMENTS)


def solution(mesh):
    in_specs = (
        P(None, None, ("sec", "dom")),
        P(("sec", "dom")),
        P(("sec", "dom")),
        P(("sec", "dom")),
        P(None, ("sec", "dom")),
    )
    out_specs = P(None, None, ("sec", "dom"))
    return jax.shard_map(local, mesh=mesh, in_specs=in_specs, out_specs=out_specs, check_vma=False)
```

```python
import functools

import jax
import jax.numpy as jnp
import numpy as np
from jax import lax
from jax.experimental import pallas as pl
from jax.experimental.pallas import tpu as pltpu
from jax.sharding import PartitionSpec as P


FACE_CAP = 24
PIECES = 3
LANES = 128
ELEMENTS = 256
ROWS = 256
TRACE_ROWS = 48
LIFT = 3.0
TIME_STEP = 0.12
SEGMENT_CARRY = [
    0.0,
    -567301805773.0 / 1357537059087.0,
    -2404267990393.0 / 2016746695238.0,
    -3550918686646.0 / 2091501179385.0,
    -1275806237668.0 / 842570457699.0,
]
SEGMENT_WEIGHTS = [
    1432997174477.0 / 9575080441755.0,
    5161836677717.0 / 13612068292357.0,
    1720146321549.0 / 2090206949498.0,
    3134564353537.0 / 4481467310338.0,
    2277821191437.0 / 14882151754819.0,
]
BF = jnp.bfloat16
F32 = jnp.float32


def node_derivative():
    points = np.array([-1.0, -1.0 / np.sqrt(5.0), 1.0 / np.sqrt(5.0), 1.0])
    products = np.array(
        [np.prod([points[row] - points[col] for col in range(4) if col != row]) for row in range(4)]
    )
    matrix = np.zeros((4, 4))
    for row in range(4):
        for col in range(4):
            if row != col:
                matrix[row, col] = products[row] / (products[col] * (points[row] - points[col]))
        matrix[row, row] = -np.sum(matrix[row])
    return matrix


def along(matrix, direction):
    eye = np.eye(4)
    parts = [eye, eye, eye]
    parts[direction] = matrix
    return np.kron(np.kron(parts[0], parts[1]), parts[2])


def face_nodes(face):
    direction, side = divmod(face, 2)
    index = np.arange(64).reshape(4, 4, 4)
    return np.take(index, 3 * side, axis=direction).reshape(-1)


def interior_matrix():
    derivative = node_derivative()
    total = np.zeros((256, 256))
    for a in range(3):
        d = along(derivative, a)
        total[0:64, 64 * (a + 1) : 64 * (a + 2)] -= d
        total[64 * (a + 1) : 64 * (a + 2), 0:64] -= d
    for face in range(6):
        a, side = divmod(face, 2)
        sign = 2.0 * side - 1.0
        nodes = face_nodes(face)
        va = 64 * (a + 1) + nodes
        total[nodes, nodes] -= LIFT
        total[nodes, va] += LIFT * sign
        total[va, va] -= LIFT
        total[va, nodes] += LIFT * sign
        for b in range(3):
            if b != a:
                vb = 64 * (b + 1) + nodes
                total[vb, vb] -= LIFT
    return total


def trace_matrix():
    total = np.zeros((6 * TRACE_ROWS, 256))
    for face in range(6):
        a, side = divmod(face, 2)
        sign = 2.0 * side - 1.0
        nodes = face_nodes(face)
        rows = TRACE_ROWS * face + np.arange(16)
        total[rows, nodes] = 1.0
        total[rows, 64 * (a + 1) + nodes] = sign
        for number, b in enumerate([b for b in range(3) if b != a]):
            total[rows + 16 * (number + 1), 64 * (b + 1) + nodes] = 1.0
    return total


def lift_matrix():
    total = np.zeros((256, 6 * TRACE_ROWS))
    for face in range(6):
        a, side = divmod(face, 2)
        sign = 2.0 * side - 1.0
        nodes = face_nodes(face)
        cols = TRACE_ROWS * face + np.arange(16)
        total[nodes, cols] = 1.0
        total[64 * (a + 1) + nodes, cols] = -sign
        for number, b in enumerate([b for b in range(3) if b != a]):
            total[64 * (b + 1) + nodes, cols + 16 * (number + 1)] = 1.0
    return total


def two_terms(matrix):
    high = matrix.astype(np.float32).astype(BF)
    low = (matrix - high.astype(np.float64)).astype(np.float32).astype(BF)
    return high, low


def mm(a, b):
    return lax.dot_general(a, b, (((1,), (0,)), ((), ())), preferred_element_type=F32)


def mm_nt(a, b):
    return lax.dot_general(a, b, (((1,), (1,)), ((), ())), preferred_element_type=F32)


def split(x):
    high = x.astype(BF)
    return high, (x - high.astype(F32)).astype(BF)


def one_hot(mask):
    return jnp.where(mask, 1.0, 0.0).astype(BF)


def lane_iota(shape):
    return lax.broadcasted_iota(jnp.int32, shape, 1)


def row_iota(shape):
    return lax.broadcasted_iota(jnp.int32, shape, 0)


def picked_traces(state, pick, kinds, trace):
    high, low = split(state)
    chosen = jnp.concatenate([mm(high, pick).astype(BF), mm(low, pick).astype(BF)], axis=1)
    shown = mm(trace, chosen)
    return of_kind(shown[:, :256] + shown[:, 256:], kinds)


def of_kind(shown, kinds):
    total = jnp.zeros((TRACE_ROWS, 256), F32)
    for face in range(6):
        part = shown[TRACE_ROWS * face : TRACE_ROWS * (face + 1)]
        total = total + jnp.where(kinds[face : face + 1] > 0, part, 0.0)
    return total


def arrived(toward, across, back):
    return across, toward + back


def by_kind(came, sent, kinds):
    far = lane_iota((TRACE_ROWS, LANES)) < PIECES * FACE_CAP
    from_left, from_right = sides(*came)
    own_left, own_right = sides(*sent)
    got = jnp.concatenate(
        [jnp.where(far, from_right, own_left), jnp.where(far, from_left, own_right)], axis=1
    )
    masked = jnp.concatenate(
        [jnp.where(kinds[face : face + 1] > 0, got, 0.0) for face in range(6)], axis=0
    )
    return jnp.concatenate(split(masked), axis=0)


def far_rates(stacks, place, lift_two):
    return mm(lift_two, mm(stacks, place).astype(BF))


def sides(first, second):
    odd = ((lax.axis_index("dom") >> 1) & 1) == 1
    return jnp.where(odd, second, first), jnp.where(odd, first, second)


def core_number():
    return lax.axis_index("dom") & 1


def chip_halves(mine, other):
    first = core_number() == 0
    return jnp.where(first, mine, other), jnp.where(first, other, mine)


def difference_along(stride):
    row, col = row_iota((64, 64)), lane_iota((64, 64))
    at, step = (row // stride) & 3, ((col // stride) & 3) - ((row // stride) & 3)
    inner = jnp.where(step == 1, 0.5, jnp.where(step == -1, -0.5, 0.0))
    lower = jnp.where(step == 1, 1.0, jnp.where(step == 0, -1.0, 0.0))
    upper = jnp.where(step == 0, 1.0, jnp.where(step == -1, -1.0, 0.0))
    value = jnp.where(at == 0, lower, jnp.where(at == 3, upper, inner))
    return jnp.where(col - row == step * stride, value, 0.0).astype(BF)


def lamb_kernel(packed, lamb_out):
    slopes = jnp.concatenate([difference_along(stride) for stride in (16, 4, 1)], axis=0)
    v = [packed[64 * a : 64 * (a + 1)] for a in range(3)]
    high, low = split(jnp.concatenate(v, axis=1))
    found = mm(slopes, high) + mm(slopes, low)

    def slope(component, direction):
        return found[64 * direction : 64 * direction + 64, 256 * component : 256 * component + 256]

    w = [
        slope(2, 1) - slope(1, 2),
        slope(0, 2) - slope(2, 0),
        slope(1, 0) - slope(0, 1),
    ]
    rho = packed[192:256]
    lamb_out[0:64] = rho * (w[1] * v[2] - w[2] * v[1])
    lamb_out[64:128] = rho * (w[2] * v[0] - w[0] * v[2])
    lamb_out[128:192] = rho * (w[0] * v[1] - w[1] * v[0])


def depart_kernel(mine, other, first_out, second_out, chip_out, select_out, keep_out, arrive_out):
    low, high = chip_halves(mine[...], other[...])
    chip_out[:, 0:256] = low
    chip_out[:, 256:512] = high
    first = (lax.axis_index("dom") & -2).astype(F32)
    spread = one_hot((lane_iota((64, 256)) >> 2) == row_iota((64, 256)))
    before = one_hot(row_iota((256, 256)) < lane_iota((256, 256)))
    row8 = row_iota((8, 256))
    wanted = jnp.where(row8 == 0, 0, jnp.where(row8 < 3, row8 - 3, row8 - 2)).astype(F32)
    members = []
    for number, half in enumerate((low, high)):
        owner = half[263:264, 0:64] - (first + number)
        owner = jnp.clip(jnp.broadcast_to(owner, (8, 64)), -8.0, 8.0).astype(BF)
        member = (mm(owner, spread) == wanted) & (row8 < 5)
        members.append(jnp.where(member, 1.0, 0.0))
    members = jnp.concatenate(members, axis=0)
    rank = mm(members.astype(BF), before)
    count = jnp.sum(members, axis=1, keepdims=True)

    def group(device, offset):
        return 8 * device + {0: 0, -2: 1, -1: 2, 1: 3, 2: 4}[offset]

    def start(device, offset):
        total = jnp.zeros((1, 1), F32)
        for number in (0, -2, -1, 1, 2):
            if number == offset:
                return total
            at = group(device, number)
            total = total + count[at : at + 1]

    def target(device, moves):
        total = jnp.full((1, 256), -1.0, F32)
        for offset, base in moves:
            at = group(device, offset)
            total = total + members[at : at + 1] * (rank[at : at + 1] + (base + 1.0))
        return total

    low_target = target(0, ((-2, 0.0), (-1, 16.0), (2, 48.0)))
    high_target = target(1, ((-2, 32.0), (1, 64.0), (2, 80.0)))
    number = row_iota((96, 256)).astype(F32)
    select = jnp.concatenate([one_hot(low_target == number), one_hot(high_target == number)], axis=1)
    select_out[...] = select
    cells = jnp.concatenate([low[0:256], high[0:256]], axis=1)
    cells_high, cells_low = split(cells)
    sent = mm_nt(select, cells_high) + mm_nt(select, cells_low)
    first_out[...], second_out[...] = sides(sent[0:48], sent[48:96])

    low_place = target(0, ((0, 0.0), (1, 256.0 + start(1, -1))))
    high_place = target(1, ((0, 256.0), (-1, start(0, 1))))
    number = row_iota((512, 256)).astype(F32)
    keep_out[:, 0:256] = one_hot(low_place == number)
    keep_out[:, 256:512] = one_hot(high_place == number)
    column = lane_iota((16, 512)).astype(F32)
    number = row_iota((16, 512)).astype(F32)
    for piece, (device, offset) in enumerate(((0, -2), (0, -1), (1, -2), (0, 2), (1, 1), (1, 2))):
        at = group(device, offset)
        begin = start(device, offset) + 256.0 * device
        arrive_out[16 * piece : 16 * piece + 16, :] = one_hot(
            (column - begin == number) & (number < count[at : at + 1])
        )


def tables_kernel(
    chip, keep,
    kept_out, local_out, place_out, own_place_out, kinds_out, pick_out, send_kinds_out, meet_out,
):
    high, low = split(chip[0:256])
    kept_out[...] = mm_nt(high, keep[...]) + mm_nt(low, keep[...])
    row = row_iota((256, 256))
    ones = jnp.ones((8, 256), BF)
    kinds = [jnp.zeros((1, 256), F32)] * 6
    places = []
    for device in range(2):
        place = jnp.zeros((256, 256), F32)
        for face in range(6):
            where = chip[256 + face : 257 + face, 256 * device : 256 * (device + 1)].astype(jnp.int32)
            local_out[6 * device + face] = one_hot(where - ELEMENTS * (face ^ 1) == row)
            n = where - 6 * ELEMENTS
            if device == 0:
                entry = jnp.where(n < 48, n + 128, jnp.where(n < 72, n + 24, n - 72))
            else:
                entry = jnp.where(n < 48, n + 176, n - 24)
            hit = jnp.where(jnp.where(n < 0, -1, entry) == row, 1.0, 0.0)
            place = place + hit
            kinds[face] = kinds[face] + mm_nt(ones, hit.astype(BF))[0:1]
        places.append(place)
    own_place_out[...] = jnp.where(core_number() == 0, places[0], places[1]).astype(BF)
    place = jnp.concatenate(places, axis=1).astype(BF)
    place_out[...] = place
    kinds_out[...] = jnp.concatenate(kinds + [jnp.zeros((2, 256), F32)], axis=0)
    lane = lane_iota((8, LANES))
    lists = [
        jnp.broadcast_to(chip[263:264, 256 * device + 128 : 256 * device + 256], (8, LANES))
        for device in range(2)
    ]
    left = jnp.where(lane < 48, lists[0], pltpu.roll(lists[1], 48, 1))
    right = jnp.where(
        lane < 24,
        pltpu.roll(lists[0], LANES - 72, 1),
        jnp.where(lane < 72, pltpu.roll(lists[1], LANES - 24, 1), pltpu.roll(lists[0], 24, 1)),
    )
    names = jnp.concatenate(
        [jnp.where(lane < 96, left, -1.0), jnp.where(lane < 96, right, -1.0)], axis=1
    ).astype(jnp.int32)
    wide = lane_iota((8, 256))
    second = ((wide >= 48) & (wide < 128)) | ((wide >= 152) & (wide < 200))
    column = jnp.where(names < 0, -1, (names & 255) + jnp.where(second, 256, 0))
    pick = one_hot(column[0:1] == row_iota((512, 256)))
    pick_out[...] = pick
    meet_out[...] = mm(place, pick).astype(BF)
    send_kinds_out[...] = jnp.where((names >> 8) == row_iota((8, 256)), 1.0, 0.0)


def arrive_kernel(
    toward, across, back, kept, arrive, pick, send_kinds, trace, state_out, first_out, second_out
):
    got = jnp.concatenate(sides(*arrived(toward[...], across[...], back[...])), axis=0)
    high, low = split(jnp.transpose(got))
    state = kept[...] + (mm(high, arrive[...]) + mm(low, arrive[...]))
    state_out[...] = state
    sent = picked_traces(state, pick[...], send_kinds[...], trace[...])
    first_out[...], second_out[...] = sides(sent[:, :LANES], sent[:, LANES:])


def force_kernel(first, second, third, packed, after, out):
    lamb = first[...] + second[...] + third[...]
    high, low = split(lamb)
    source = one_hot(packed[262:263].astype(jnp.int32) == row_iota((256, 256)))
    out[...] = mm(high, source) + mm(low, source)


def force_depart_kernel(
    mine, other, select, keep, own_first, own_second, first_out, second_out, kept_out
):
    force = jnp.concatenate(chip_halves(mine[...], other[...]), axis=1)
    high, low = split(force)
    sent = mm_nt(select[...], high) + mm_nt(select[...], low)
    pieces = sides(sent[0:48], sent[48:96])
    for out, piece, own in ((first_out, pieces[0], own_first), (second_out, pieces[1], own_second)):
        out[:, 0:192] = piece
        out[:, 192:256] = jnp.zeros((48, 64), F32)
        out[:, 256:384] = own[...]
    kept_out[...] = mm_nt(high, keep[...]) + mm_nt(low, keep[...])


def near_rates(state, near, interior, trace, lift_two):
    high, low = split(state)
    rates = mm(interior, jnp.concatenate([high, low, high], axis=0))
    shown = mm(trace, jnp.concatenate([high, low], axis=1))
    shown_high, shown_low = split(shown[:, 0:512] + shown[:, 512:1024])
    faces = []
    for device in range(2):
        columns = slice(256 * device, 256 * (device + 1))
        outside_high, outside_low = [], []
        for face in range(6):
            rows = slice(TRACE_ROWS * (face ^ 1), TRACE_ROWS * (face ^ 1) + TRACE_ROWS)
            stacked = jnp.concatenate([shown_high[rows, columns], shown_low[rows, columns]], axis=0)
            found = mm(stacked, near[6 * device + face]).astype(BF)
            outside_high.append(found[:TRACE_ROWS])
            outside_low.append(found[TRACE_ROWS:])
        faces.append(jnp.concatenate(outside_high + outside_low, axis=0))
    return rates + LIFT * mm(lift_two, jnp.concatenate(faces, axis=1))


def weight_of(segment):
    acoustic = lax.axis_index("sec") > 0
    return jnp.where(acoustic, F32(SEGMENT_WEIGHTS[segment]), F32(0.0))


def first_inner_kernel(state, near, interior, trace, lift_two, carry_out):
    carry_out[...] = TIME_STEP * near_rates(
        state[...], near, interior[...], trace[...], lift_two[...]
    )


def first_outer_kernel(
    toward, across, back, sent_first, sent_second, state, carry, kinds, place, lift_two,
    kept_force, arrive, pick, send_kinds, trace,
    state_out, carry_out, first_out, second_out, force_out,
):
    came = arrived(toward[...], across[...], back[...])
    stacks = by_kind(
        (came[0][:, 256:384], came[1][:, 256:384]), (sent_first[...], sent_second[...]), kinds[...]
    )
    rates = far_rates(stacks, place[...], lift_two[...])
    got = jnp.concatenate(sides(came[0][:, 0:256], came[1][:, 0:256]), axis=0)
    high, low = split(jnp.transpose(got)[0:192])
    force = kept_force[...] + (mm(high, arrive[...]) + mm(low, arrive[...]))
    force_out[...] = force
    carry_now = carry[...] + (LIFT * TIME_STEP) * rates
    carry_now = jnp.concatenate([carry_now[0:64], carry_now[64:256] + TIME_STEP * force], axis=0)
    state_now = state[...] + weight_of(0) * carry_now
    state_out[...] = state_now
    carry_out[...] = carry_now
    sent = picked_traces(state_now, pick[...], send_kinds[...], trace[...])
    first_out[...], second_out[...] = sides(sent[:, :LANES], sent[:, LANES:])


def inner_kernel(segment, state, carry, force, near, interior, trace, lift_two, *refs):
    if segment == 1:
        state_now, carry_now = state[...], carry[...]
    else:
        (stacks, place), refs = refs[:2], refs[2:]
        rates = far_rates(stacks[...], place[...], lift_two[...])
        carry_now = carry[...] + (LIFT * TIME_STEP) * rates
        state_now = state[...] + weight_of(segment - 1) * carry_now
    rates = near_rates(state_now, near, interior[...], trace[...], lift_two[...])
    own = SEGMENT_CARRY[segment] * carry_now + TIME_STEP * rates
    own = jnp.concatenate([own[0:64], own[64:256] + TIME_STEP * force[...]], axis=0)
    ahead = state_now + weight_of(segment) * own
    if segment == 4:
        refs[0][...] = jnp.where(core_number() == 0, ahead[:, 0:256], ahead[:, 256:512])
        return
    pick, send_kinds, state_out, carry_out, base_out = refs
    state_out[...] = state_now
    carry_out[...] = own
    base_out[...] = picked_traces(ahead, pick[...], send_kinds[...], trace[...])


def outer_kernel(
    segment, toward, across, back, sent_first, sent_second, kinds, meet, reach, send_kinds, base,
    stacks_out, first_out, second_out,
):
    stacks = by_kind(
        arrived(toward[...], across[...], back[...]), (sent_first[...], sent_second[...]), kinds[...]
    )
    stacks_out[...] = stacks
    shown = mm(reach[...], mm(stacks, meet[...]).astype(BF))
    sent = base[...] + (weight_of(segment) * F32(LIFT * TIME_STEP)) * of_kind(shown, send_kinds[...])
    first_out[...], second_out[...] = sides(sent[:, :LANES], sent[:, LANES:])


def last_kernel(
    toward, across, back, sent_first, sent_second, kinds, own_place, lift_two, ahead, out
):
    stacks = by_kind(
        arrived(toward[...], across[...], back[...]), (sent_first[...], sent_second[...]), kinds[...]
    )
    rates = far_rates(stacks, own_place[...], lift_two[...])
    out[...] = ahead[...] + (weight_of(4) * F32(LIFT * TIME_STEP)) * rates


def call(kernel, outs, *args, flops=1 << 20):
    vmem = pl.BlockSpec(memory_space=pltpu.VMEM)
    size = sum(int(np.prod(a.shape)) * a.dtype.itemsize for a in (*args, *outs))
    return pl.pallas_call(
        kernel,
        out_shape=list(outs),
        in_specs=[vmem] * len(args),
        out_specs=[vmem] * len(outs),
        compiler_params=pltpu.CompilerParams(vmem_limit_bytes=32 << 20),
        cost_estimate=pl.CostEstimate(flops=flops, bytes_accessed=size, transcendentals=0),
    )(*args)


def arr(*shape, dtype=F32):
    return jax.ShapeDtypeStruct(shape, dtype)


def trade(first, second, sections):
    count = lax.axis_size("dom")
    toward, across, back = [], [], []
    for section in sections:
        for dom in range(count - 2):
            chip, low = dom >> 1, section * count + dom
            if chip & 1:
                across += [(low, low + 2), (low + 2, low)]
            elif chip & 2:
                toward.append((low, low + 2))
                back.append((low + 2, low))
            else:
                toward.append((low + 2, low))
                back.append((low, low + 2))
    came = []
    for value, pairs in ((second, toward), (first, across), (second, back)):
        came.append(lax.ppermute(value, ("sec", "dom"), pairs))
    return came


def swap(value):
    return lax.ppermute(value, "dom", [(at, at ^ 1) for at in range(lax.axis_size("dom"))])


def step(fields, source_map, new_owner, send_list, face_slot):
    cells = fields.reshape(ROWS, ELEMENTS)
    high, low = two_terms(interior_matrix())
    interior = jnp.asarray(np.concatenate([high, high, low], axis=1))
    trace = jnp.asarray(trace_matrix().astype(BF))
    lift_two = jnp.asarray(np.concatenate([lift_matrix()] * 2, axis=1).astype(BF))
    reach = jnp.asarray(np.concatenate([trace_matrix() @ lift_matrix()] * 2, axis=1).astype(BF))
    every = range(lax.axis_size("sec"))
    acoustic = every[1:]
    piece, whole = arr(TRACE_ROWS, LANES), arr(256, 512)

    names = jnp.zeros((264, 256), jnp.int32)
    for part, row, lane in (
        (face_slot, 256, 0),
        (source_map.reshape(1, 256), 262, 0),
        (new_owner.reshape(1, 64), 263, 0),
        (send_list.reshape(1, 96), 263, 128),
    ):
        rows, lanes = part.shape
        edges = ((row, 264 - row - rows, 0), (lane, 256 - lane - lanes, 0))
        names = names + lax.pad(part, jnp.int32(0), edges)
    packed = names.astype(F32) + lax.pad(cells, F32(0.0), ((0, 8, 0), (0, 0, 0)))
    (lamb,) = call(lamb_kernel, [arr(192, 256)], packed)
    lamb_parts = []
    for section in (1, 2, 3):
        lamb_parts.append(lax.ppermute(lamb, "sec", [(0, section)]))
    other = swap(packed)
    *leaving, chip, select, keep, arrive = call(
        depart_kernel,
        [
            arr(48, 256),
            arr(48, 256),
            arr(264, 512),
            arr(96, 512, dtype=BF),
            arr(512, 512, dtype=BF),
            arr(96, 512, dtype=BF),
        ],
        packed,
        other,
    )
    moved = trade(*leaving, every)
    kept, near, place, own_place, kinds, pick, send_kinds, meet = call(
        tables_kernel,
        [
            whole,
            arr(12, 256, 256, dtype=BF),
            arr(256, 512, dtype=BF),
            arr(256, 256, dtype=BF),
            arr(8, 256),
            arr(512, 256, dtype=BF),
            arr(8, 256),
            arr(256, 256, dtype=BF),
        ],
        chip,
        keep,
    )
    (force_mine,) = call(force_kernel, [arr(192, 256)], *lamb_parts, packed, kinds)
    force_other = swap(force_mine)
    state, *sent = call(
        arrive_kernel, [whole, piece, piece], *moved, kept, arrive, pick, send_kinds, trace
    )
    *wide, kept_force = call(
        force_depart_kernel,
        [arr(48, 384), arr(48, 384), arr(192, 512)],
        force_mine, force_other, select, keep, *sent,
    )
    came = trade(*wide, acoustic)
    (carry,) = call(first_inner_kernel, [whole], state, near, interior, trace, lift_two)
    state, carry, *later, force = call(
        first_outer_kernel,
        [whole, whole, piece, piece, arr(192, 512)],
        *came, *sent, state, carry, kinds, place, lift_two, kept_force, arrive, pick, send_kinds, trace,
    )
    stacks = None
    for segment in range(1, 5):
        sent, came = later, trade(*later, acoustic)
        args = [state, carry, force, near, interior, trace, lift_two]
        if segment > 1:
            args += [stacks, place]
        if segment == 4:
            (ahead,) = call(functools.partial(inner_kernel, segment), [arr(256, 256)], *args)
            break
        state, carry, base = call(
            functools.partial(inner_kernel, segment),
            [whole, whole, arr(TRACE_ROWS, 256)],
            *args, pick, send_kinds,
        )
        stacks, *later = call(
            functools.partial(outer_kernel, segment),
            [arr(12 * TRACE_ROWS, 256, dtype=BF), piece, piece],
            *came, *sent, kinds, meet, reach, send_kinds, base,
        )
    (out,) = call(
        last_kernel, [arr(256, 256)], *came, *sent, kinds, own_place, lift_two, ahead
    )
    return out.reshape(4, 64, ELEMENTS)


def solution(mesh):
    in_specs = (
        P(None, None, ("sec", "dom")),
        P(("sec", "dom")),
        P(("sec", "dom")),
        P(("sec", "dom")),
        P(None, ("sec", "dom")),
    )
    out_specs = P(None, None, ("sec", "dom"))
    return jax.shard_map(step, mesh=mesh, in_specs=in_specs, out_specs=out_specs, check_vma=False)
```

```python
import functools

import jax
import jax.numpy as jnp
import numpy as np
from jax import lax
from jax.experimental import pallas as pl
from jax.experimental.pallas import tpu as pltpu
from jax.sharding import PartitionSpec as P


FACE_CAP = 24
PIECES = 3
LANES = 128
ELEMENTS = 256
ROWS = 256
TRACE_ROWS = 48
LIFT = 3.0
TIME_STEP = 0.12
SEGMENT_CARRY = [
    0.0,
    -567301805773.0 / 1357537059087.0,
    -2404267990393.0 / 2016746695238.0,
    -3550918686646.0 / 2091501179385.0,
    -1275806237668.0 / 842570457699.0,
]
SEGMENT_WEIGHTS = [
    1432997174477.0 / 9575080441755.0,
    5161836677717.0 / 13612068292357.0,
    1720146321549.0 / 2090206949498.0,
    3134564353537.0 / 4481467310338.0,
    2277821191437.0 / 14882151754819.0,
]
BF = jnp.bfloat16
F32 = jnp.float32


def node_derivative():
    points = np.array([-1.0, -1.0 / np.sqrt(5.0), 1.0 / np.sqrt(5.0), 1.0])
    products = np.array(
        [np.prod([points[row] - points[col] for col in range(4) if col != row]) for row in range(4)]
    )
    matrix = np.zeros((4, 4))
    for row in range(4):
        for col in range(4):
            if row != col:
                matrix[row, col] = products[row] / (products[col] * (points[row] - points[col]))
        matrix[row, row] = -np.sum(matrix[row])
    return matrix


def along(matrix, direction):
    eye = np.eye(4)
    parts = [eye, eye, eye]
    parts[direction] = matrix
    return np.kron(np.kron(parts[0], parts[1]), parts[2])


def face_nodes(face):
    direction, side = divmod(face, 2)
    index = np.arange(64).reshape(4, 4, 4)
    return np.take(index, 3 * side, axis=direction).reshape(-1)


def interior_matrix():
    derivative = node_derivative()
    total = np.zeros((256, 256))
    for a in range(3):
        d = along(derivative, a)
        total[0:64, 64 * (a + 1) : 64 * (a + 2)] -= d
        total[64 * (a + 1) : 64 * (a + 2), 0:64] -= d
    for face in range(6):
        a, side = divmod(face, 2)
        sign = 2.0 * side - 1.0
        nodes = face_nodes(face)
        va = 64 * (a + 1) + nodes
        total[nodes, nodes] -= LIFT
        total[nodes, va] += LIFT * sign
        total[va, va] -= LIFT
        total[va, nodes] += LIFT * sign
        for b in range(3):
            if b != a:
                vb = 64 * (b + 1) + nodes
                total[vb, vb] -= LIFT
    return total


def trace_matrix():
    total = np.zeros((6 * TRACE_ROWS, 256))
    for face in range(6):
        a, side = divmod(face, 2)
        sign = 2.0 * side - 1.0
        nodes = face_nodes(face)
        rows = TRACE_ROWS * face + np.arange(16)
        total[rows, nodes] = 1.0
        total[rows, 64 * (a + 1) + nodes] = sign
        for number, b in enumerate([b for b in range(3) if b != a]):
            total[rows + 16 * (number + 1), 64 * (b + 1) + nodes] = 1.0
    return total


def lift_matrix():
    total = np.zeros((256, 6 * TRACE_ROWS))
    for face in range(6):
        a, side = divmod(face, 2)
        sign = 2.0 * side - 1.0
        nodes = face_nodes(face)
        cols = TRACE_ROWS * face + np.arange(16)
        total[nodes, cols] = 1.0
        total[64 * (a + 1) + nodes, cols] = -sign
        for number, b in enumerate([b for b in range(3) if b != a]):
            total[64 * (b + 1) + nodes, cols + 16 * (number + 1)] = 1.0
    return total


def two_terms(matrix):
    high = matrix.astype(np.float32).astype(BF)
    low = (matrix - high.astype(np.float64)).astype(np.float32).astype(BF)
    return high, low


def mm(a, b):
    return lax.dot_general(a, b, (((1,), (0,)), ((), ())), preferred_element_type=F32)


def mm_nt(a, b):
    return lax.dot_general(a, b, (((1,), (1,)), ((), ())), preferred_element_type=F32)


def split(x):
    high = x.astype(BF)
    return high, (x - high.astype(F32)).astype(BF)


def one_hot(mask):
    return jnp.where(mask, 1.0, 0.0).astype(BF)


def lane_iota(shape):
    return lax.broadcasted_iota(jnp.int32, shape, 1)


def row_iota(shape):
    return lax.broadcasted_iota(jnp.int32, shape, 0)


def picked_traces(state, pick, kinds, trace):
    high, low = split(state)
    chosen = jnp.concatenate([mm(high, pick).astype(BF), mm(low, pick).astype(BF)], axis=1)
    shown = mm(trace, chosen)
    return of_kind(shown[:, :256] + shown[:, 256:], kinds)


def of_kind(shown, kinds):
    total = jnp.zeros((TRACE_ROWS, 256), F32)
    for face in range(6):
        part = shown[TRACE_ROWS * face : TRACE_ROWS * (face + 1)]
        total = total + jnp.where(kinds[face : face + 1] > 0, part, 0.0)
    return total


def by_kind(came, sent, kinds):
    far = lane_iota((TRACE_ROWS, LANES)) < PIECES * FACE_CAP
    from_left, from_right = sides(*came)
    own_left, own_right = sides(*sent)
    got = jnp.concatenate(
        [jnp.where(far, from_right, own_left), jnp.where(far, from_left, own_right)], axis=1
    )
    masked = jnp.concatenate(
        [jnp.where(kinds[face : face + 1] > 0, got, 0.0) for face in range(6)], axis=0
    )
    return jnp.concatenate(split(masked), axis=0)


def far_rates(stacks, place, lift_two):
    return mm(lift_two, mm(stacks, place).astype(BF))


def sides(first, second):
    odd = ((lax.axis_index("dom") >> 1) & 1) == 1
    return jnp.where(odd, second, first), jnp.where(odd, first, second)


def core_number():
    return lax.axis_index("dom") & 1


def chip_halves(mine, other):
    first = core_number() == 0
    return jnp.where(first, mine, other), jnp.where(first, other, mine)


def difference_along(stride):
    row, col = row_iota((64, 64)), lane_iota((64, 64))
    at, step = (row // stride) & 3, ((col // stride) & 3) - ((row // stride) & 3)
    inner = jnp.where(step == 1, 0.5, jnp.where(step == -1, -0.5, 0.0))
    lower = jnp.where(step == 1, 1.0, jnp.where(step == 0, -1.0, 0.0))
    upper = jnp.where(step == 0, 1.0, jnp.where(step == -1, -1.0, 0.0))
    value = jnp.where(at == 0, lower, jnp.where(at == 3, upper, inner))
    return jnp.where(col - row == step * stride, value, 0.0).astype(BF)


def lamb_kernel(packed, lamb_out):
    slopes = jnp.concatenate([difference_along(stride) for stride in (16, 4, 1)], axis=0)
    v = [packed[64 * a : 64 * (a + 1)] for a in range(3)]
    high, low = split(jnp.concatenate(v, axis=1))
    found = mm(slopes, high) + mm(slopes, low)

    def slope(component, direction):
        return found[64 * direction : 64 * direction + 64, 256 * component : 256 * component + 256]

    w = [
        slope(2, 1) - slope(1, 2),
        slope(0, 2) - slope(2, 0),
        slope(1, 0) - slope(0, 1),
    ]
    rho = packed[192:256]
    lamb_out[0:64] = rho * (w[1] * v[2] - w[2] * v[1])
    lamb_out[64:128] = rho * (w[2] * v[0] - w[0] * v[2])
    lamb_out[128:192] = rho * (w[0] * v[1] - w[1] * v[0])


def group_of(device, offset):
    return 8 * device + {0: 0, -2: 1, -1: 2, 1: 3, 2: 4}[offset]


def start_of(count, device, offset):
    total = jnp.zeros((1, 1), F32)
    for number in (0, -2, -1, 1, 2):
        if number == offset:
            return total
        at = group_of(device, number)
        total = total + count[at : at + 1]


def target_of(members, rank, device, moves):
    total = jnp.full((1, 256), -1.0, F32)
    for offset, base in moves:
        at = group_of(device, offset)
        total = total + members[at : at + 1] * (rank[at : at + 1] + (base + 1.0))
    return total


def depart_kernel(mine, other, first_out, second_out, select_out, ranks_out):
    low, high = chip_halves(mine[...], other[...])
    first = (lax.axis_index("dom") & -2).astype(F32)
    spread = one_hot((lane_iota((64, 256)) >> 2) == row_iota((64, 256)))
    before = one_hot(row_iota((256, 256)) < lane_iota((256, 256)))
    row8 = row_iota((8, 256))
    wanted = jnp.where(row8 == 0, 0, jnp.where(row8 < 3, row8 - 3, row8 - 2)).astype(F32)
    members = []
    for number, half in enumerate((low, high)):
        owner = half[263:264, 0:64] - (first + number)
        owner = jnp.clip(jnp.broadcast_to(owner, (8, 64)), -8.0, 8.0).astype(BF)
        member = (mm(owner, spread) == wanted) & (row8 < 5)
        members.append(jnp.where(member, 1.0, 0.0))
    members = jnp.concatenate(members, axis=0)
    rank = mm(members.astype(BF), before)
    ranks_out[0:16] = members
    ranks_out[16:32] = rank
    low_target = target_of(members, rank, 0, ((-2, 0.0), (-1, 16.0), (2, 48.0)))
    high_target = target_of(members, rank, 1, ((-2, 32.0), (1, 64.0), (2, 80.0)))
    number = row_iota((96, 256)).astype(F32)
    select = jnp.concatenate([one_hot(low_target == number), one_hot(high_target == number)], axis=1)
    select_out[...] = select
    cells = jnp.concatenate([low[0:256], high[0:256]], axis=1)
    cells_high, cells_low = split(cells)
    sent = mm_nt(select, cells_high) + mm_nt(select, cells_low)
    first_out[...], second_out[...] = sides(sent[0:48], sent[48:96])


def places_kernel(
    mine, other, ranks, trace,
    kept_out, keep_out, arrive_out, pick_out, send_kinds_out, arrive_pick_out, base_out,
):
    low, high = chip_halves(mine[...], other[...])
    members, rank = ranks[0:16], ranks[16:32]
    count = jnp.sum(members, axis=1, keepdims=True)
    low_place = target_of(members, rank, 0, ((0, 0.0), (1, 256.0 + start_of(count, 1, -1))))
    high_place = target_of(members, rank, 1, ((0, 256.0), (-1, start_of(count, 0, 1))))
    number = row_iota((512, 256)).astype(F32)
    keep = jnp.concatenate([one_hot(low_place == number), one_hot(high_place == number)], axis=1)
    keep_out[...] = keep
    column = lane_iota((16, 512)).astype(F32)
    number = row_iota((16, 512)).astype(F32)
    blocks = []
    for device, offset in ((0, -2), (0, -1), (1, -2), (0, 2), (1, 1), (1, 2)):
        at = group_of(device, offset)
        begin = start_of(count, device, offset) + 256.0 * device
        blocks.append(one_hot((column - begin == number) & (number < count[at : at + 1])))
    arrive = jnp.concatenate(blocks, axis=0)
    arrive_out[...] = arrive
    cells_high, cells_low = split(jnp.concatenate([low[0:256], high[0:256]], axis=1))
    kept = mm_nt(cells_high, keep) + mm_nt(cells_low, keep)
    kept_out[...] = kept
    lane = lane_iota((8, LANES))
    lists = [jnp.broadcast_to(half[263:264, 128:256], (8, LANES)) for half in (low, high)]
    left = jnp.where(lane < 48, lists[0], pltpu.roll(lists[1], 48, 1))
    right = jnp.where(
        lane < 24,
        pltpu.roll(lists[0], LANES - 72, 1),
        jnp.where(lane < 72, pltpu.roll(lists[1], LANES - 24, 1), pltpu.roll(lists[0], 24, 1)),
    )
    names = jnp.concatenate(
        [jnp.where(lane < 96, left, -1.0), jnp.where(lane < 96, right, -1.0)], axis=1
    ).astype(jnp.int32)
    wide = lane_iota((8, 256))
    second = ((wide >= 48) & (wide < 128)) | ((wide >= 152) & (wide < 200))
    column = jnp.where(names < 0, -1, (names & 255) + jnp.where(second, 256, 0))
    pick = one_hot(column[0:1] == row_iota((512, 256)))
    pick_out[...] = pick
    send_kinds = jnp.where((names >> 8) == row_iota((8, 256)), 1.0, 0.0)
    send_kinds_out[...] = send_kinds
    arrive_pick_out[...] = mm(arrive, pick).astype(BF)
    base_out[...] = picked_traces(kept, pick, send_kinds, trace[...])


def faces_kernel(mine, other, pick, local_out, place_out, own_place_out, kinds_out, meet_out):
    row = row_iota((256, 256))
    ones = jnp.ones((8, 256), BF)
    kinds = [jnp.zeros((1, 256), F32)] * 6
    places = []
    for device, half in enumerate(chip_halves(mine[256:264], other[256:264])):
        place = jnp.zeros((256, 256), F32)
        for face in range(6):
            where = half[face : face + 1].astype(jnp.int32)
            local_out[6 * device + face] = one_hot(where - ELEMENTS * (face ^ 1) == row)
            n = where - 6 * ELEMENTS
            if device == 0:
                entry = jnp.where(n < 48, n + 128, jnp.where(n < 72, n + 24, n - 72))
            else:
                entry = jnp.where(n < 48, n + 176, n - 24)
            hit = jnp.where(jnp.where(n < 0, -1, entry) == row, 1.0, 0.0)
            place = place + hit
            kinds[face] = kinds[face] + mm_nt(ones, hit.astype(BF))[0:1]
        places.append(place)
    own_place_out[...] = jnp.where(core_number() == 0, places[0], places[1]).astype(BF)
    place = jnp.concatenate(places, axis=1).astype(BF)
    place_out[...] = place
    kinds_out[...] = jnp.concatenate(kinds + [jnp.zeros((2, 256), F32)], axis=0)
    meet_out[...] = mm(place, pick[...]).astype(BF)


def force_kernel(first, second, third, packed, after, out):
    lamb = first[...] + second[...] + third[...]
    high, low = split(lamb)
    source = one_hot(packed[262:263].astype(jnp.int32) == row_iota((256, 256)))
    out[...] = mm(high, source) + mm(low, source)


def came_columns(first, second):
    return split(jnp.transpose(jnp.concatenate(sides(first, second), axis=0)))


def leave_kernel(
    first, second, base, arrive_pick, send_kinds, trace, force_mine, force_other, select,
    wide_first, wide_second, own_first, own_second,
):
    chosen = [mm(term, arrive_pick[...]).astype(BF) for term in came_columns(first[...], second[...])]
    shown = mm(trace[...], jnp.concatenate(chosen, axis=1))
    sent = base[...] + of_kind(shown[:, :256] + shown[:, 256:], send_kinds[...])
    own = sides(sent[:, :LANES], sent[:, LANES:])
    force = jnp.concatenate(chip_halves(force_mine[...], force_other[...]), axis=1)
    high, low = split(force)
    moved = mm_nt(select[...], high) + mm_nt(select[...], low)
    pieces = sides(moved[0:48], moved[48:96])
    for wide, piece, part in zip((wide_first, wide_second), pieces, own):
        wide[:, 0:192] = piece
        wide[:, 192:256] = jnp.zeros((48, 64), F32)
        wide[:, 256:384] = part
    own_first[...], own_second[...] = own


def near_rates(state, near, interior, trace, lift_two):
    high, low = split(state)
    rates = mm(interior, jnp.concatenate([high, low, high], axis=0))
    shown = mm(trace, jnp.concatenate([high, low], axis=1))
    shown_high, shown_low = split(shown[:, 0:512] + shown[:, 512:1024])
    faces = []
    for device in range(2):
        columns = slice(256 * device, 256 * (device + 1))
        outside_high, outside_low = [], []
        for face in range(6):
            rows = slice(TRACE_ROWS * (face ^ 1), TRACE_ROWS * (face ^ 1) + TRACE_ROWS)
            stacked = jnp.concatenate([shown_high[rows, columns], shown_low[rows, columns]], axis=0)
            found = mm(stacked, near[6 * device + face]).astype(BF)
            outside_high.append(found[:TRACE_ROWS])
            outside_low.append(found[TRACE_ROWS:])
        faces.append(jnp.concatenate(outside_high + outside_low, axis=0))
    return rates + LIFT * mm(lift_two, jnp.concatenate(faces, axis=1))


def weight_of(segment):
    acoustic = lax.axis_index("sec") > 0
    return jnp.where(acoustic, F32(SEGMENT_WEIGHTS[segment]), F32(0.0))


def first_inner_kernel(
    first, second, kept, arrive, force_mine, force_other, keep, near, interior, trace, lift_two,
    pick, send_kinds, state_out, carry_out, force_out, base_out,
):
    high, low = came_columns(first[...], second[...])
    state = kept[...] + (mm(high, arrive[...]) + mm(low, arrive[...]))
    state_out[...] = state
    high, low = split(jnp.concatenate(chip_halves(force_mine[...], force_other[...]), axis=1))
    force = mm_nt(high, keep[...]) + mm_nt(low, keep[...])
    force_out[...] = force
    own = TIME_STEP * near_rates(state, near, interior[...], trace[...], lift_two[...])
    own = jnp.concatenate([own[0:64], own[64:256] + TIME_STEP * force], axis=0)
    carry_out[...] = own
    ahead = state + weight_of(0) * own
    base_out[...] = picked_traces(ahead, pick[...], send_kinds[...], trace[...])


def first_outer_kernel(
    first, second, sent_first, sent_second, kinds, meet, reach, send_kinds, base, trace, arrive_pick,
    stacks_out, first_out, second_out,
):
    stacks = by_kind(
        (first[:, 256:384], second[:, 256:384]), (sent_first[...], sent_second[...]), kinds[...]
    )
    stacks_out[...] = stacks
    shown = LIFT * mm(reach[...], mm(stacks, meet[...]).astype(BF))
    chosen = [
        jnp.concatenate([jnp.zeros((64, 256), BF), mm(term[0:192], arrive_pick[...]).astype(BF)], axis=0)
        for term in came_columns(first[:, 0:256], second[:, 0:256])
    ]
    pushed = mm(trace[...], jnp.concatenate(chosen, axis=1))
    shown = shown + (pushed[:, :256] + pushed[:, 256:])
    sent = base[...] + (weight_of(0) * F32(TIME_STEP)) * of_kind(shown, send_kinds[...])
    first_out[...], second_out[...] = sides(sent[:, :LANES], sent[:, LANES:])


def inner_kernel(segment, state, carry, force, stacks, place, near, interior, trace, lift_two, *refs):
    rates = far_rates(stacks[...], place[...], lift_two[...])
    carry_now = carry[...] + (LIFT * TIME_STEP) * rates
    force = force[...]
    if segment == 1:
        (first, second, arrive), refs = refs[:3], refs[3:]
        high, low = came_columns(first[:, 0:256], second[:, 0:256])
        came = mm(high[0:192], arrive[...]) + mm(low[0:192], arrive[...])
        carry_now = jnp.concatenate([carry_now[0:64], carry_now[64:256] + TIME_STEP * came], axis=0)
        force = force + came
    state_now = state[...] + weight_of(segment - 1) * carry_now
    rates = near_rates(state_now, near, interior[...], trace[...], lift_two[...])
    own = SEGMENT_CARRY[segment] * carry_now + TIME_STEP * rates
    own = jnp.concatenate([own[0:64], own[64:256] + TIME_STEP * force], axis=0)
    ahead = state_now + weight_of(segment) * own
    if segment == 4:
        refs[0][...] = jnp.where(core_number() == 0, ahead[:, 0:256], ahead[:, 256:512])
        return
    (pick, send_kinds, state_out, carry_out, base_out), refs = refs[:5], refs[5:]
    state_out[...] = state_now
    carry_out[...] = own
    base_out[...] = picked_traces(ahead, pick[...], send_kinds[...], trace[...])
    if segment == 1:
        refs[0][...] = force


def outer_kernel(
    segment, first, second, sent_first, sent_second, kinds, meet, reach, send_kinds, base,
    stacks_out, first_out, second_out,
):
    stacks = by_kind((first[...], second[...]), (sent_first[...], sent_second[...]), kinds[...])
    stacks_out[...] = stacks
    shown = mm(reach[...], mm(stacks, meet[...]).astype(BF))
    sent = base[...] + (weight_of(segment) * F32(LIFT * TIME_STEP)) * of_kind(shown, send_kinds[...])
    first_out[...], second_out[...] = sides(sent[:, :LANES], sent[:, LANES:])


def last_kernel(first, second, sent_first, sent_second, kinds, own_place, lift_two, ahead, out):
    stacks = by_kind((first[...], second[...]), (sent_first[...], sent_second[...]), kinds[...])
    rates = far_rates(stacks, own_place[...], lift_two[...])
    out[...] = ahead[...] + (weight_of(4) * F32(LIFT * TIME_STEP)) * rates


def call(kernel, outs, *args, flops=1 << 20):
    vmem = pl.BlockSpec(memory_space=pltpu.VMEM)
    size = sum(int(np.prod(a.shape)) * a.dtype.itemsize for a in (*args, *outs))
    return pl.pallas_call(
        kernel,
        out_shape=list(outs),
        in_specs=[vmem] * len(args),
        out_specs=[vmem] * len(outs),
        compiler_params=pltpu.CompilerParams(vmem_limit_bytes=32 << 20),
        cost_estimate=pl.CostEstimate(flops=flops, bytes_accessed=size, transcendentals=0),
    )(*args)


def arr(*shape, dtype=F32):
    return jax.ShapeDtypeStruct(shape, dtype)


def trade(first, second, sections):
    count = lax.axis_size("dom")
    came = []
    for value, odd in ((first, 1), (second, 0)):
        pairs = []
        for section in sections:
            for dom in range(count - 2):
                if (dom >> 1) & 1 == odd:
                    low = section * count + dom
                    pairs += [(low, low + 2), (low + 2, low)]
        came.append(lax.ppermute(value, ("sec", "dom"), pairs))
    return came


def swap(value):
    return lax.ppermute(value, "dom", [(at, at ^ 1) for at in range(lax.axis_size("dom"))])


def step(fields, source_map, new_owner, send_list, face_slot):
    cells = fields.reshape(ROWS, ELEMENTS)
    high, low = two_terms(interior_matrix())
    interior = jnp.asarray(np.concatenate([high, high, low], axis=1))
    trace = jnp.asarray(trace_matrix().astype(BF))
    lift_two = jnp.asarray(np.concatenate([lift_matrix()] * 2, axis=1).astype(BF))
    reach = jnp.asarray(np.concatenate([trace_matrix() @ lift_matrix()] * 2, axis=1).astype(BF))
    every = range(lax.axis_size("sec"))
    acoustic = every[1:]
    piece, whole = arr(TRACE_ROWS, LANES), arr(256, 512)

    names = jnp.zeros((264, 256), jnp.int32)
    for part, row, lane in (
        (face_slot, 256, 0),
        (source_map.reshape(1, 256), 262, 0),
        (new_owner.reshape(1, 64), 263, 0),
        (send_list.reshape(1, 96), 263, 128),
    ):
        rows, lanes = part.shape
        edges = ((row, 264 - row - rows, 0), (lane, 256 - lane - lanes, 0))
        names = names + lax.pad(part, jnp.int32(0), edges)
    packed = names.astype(F32) + lax.pad(cells, F32(0.0), ((0, 8, 0), (0, 0, 0)))
    (lamb,) = call(lamb_kernel, [arr(192, 256)], packed)
    lamb_parts = []
    for section in (1, 2, 3):
        lamb_parts.append(lax.ppermute(lamb, "sec", [(0, section)]))
    other = swap(packed)
    *leaving, select, ranks = call(
        depart_kernel,
        [arr(48, 256), arr(48, 256), arr(96, 512, dtype=BF), arr(32, 256)],
        packed,
        other,
    )
    moved = trade(*leaving, every)
    kept, keep, arrive, pick, send_kinds, arrive_pick, base = call(
        places_kernel,
        [
            whole,
            arr(512, 512, dtype=BF),
            arr(96, 512, dtype=BF),
            arr(512, 256, dtype=BF),
            arr(8, 256),
            arr(96, 256, dtype=BF),
            arr(TRACE_ROWS, 256),
        ],
        packed,
        other,
        ranks,
        trace,
    )
    (force_mine,) = call(force_kernel, [arr(192, 256)], *lamb_parts, packed, send_kinds)
    force_other = swap(force_mine)
    *wide, own_first, own_second = call(
        leave_kernel,
        [arr(48, 384), arr(48, 384), piece, piece],
        *moved, base, arrive_pick, send_kinds, trace, force_mine, force_other, select,
    )
    sent = [own_first, own_second]
    came = trade(*wide, acoustic)
    near, place, own_place, kinds, meet = call(
        faces_kernel,
        [
            arr(12, 256, 256, dtype=BF),
            arr(256, 512, dtype=BF),
            arr(256, 256, dtype=BF),
            arr(8, 256),
            arr(256, 256, dtype=BF),
        ],
        packed,
        other,
        pick,
    )
    state, carry, force, base = call(
        first_inner_kernel,
        [whole, whole, arr(192, 512), arr(TRACE_ROWS, 256)],
        *moved, kept, arrive, force_mine, force_other, keep, near, interior, trace, lift_two,
        pick, send_kinds,
    )
    sending = [arr(12 * TRACE_ROWS, 256, dtype=BF), piece, piece]
    stacks, *later = call(
        first_outer_kernel,
        sending,
        *came, *sent, kinds, meet, reach, send_kinds, base, trace, arrive_pick,
    )
    extra = [*came, arrive]
    for segment in range(1, 5):
        sent, came = later, trade(*later, acoustic)
        inner = functools.partial(inner_kernel, segment)
        args = [state, carry, force, stacks, place, near, interior, trace, lift_two]
        if segment == 4:
            (ahead,) = call(inner, [arr(256, 256)], *args)
            break
        outs = [whole, whole, arr(TRACE_ROWS, 256)]
        if segment == 1:
            state, carry, base, force = call(
                inner, [*outs, arr(192, 512)], *args, *extra, pick, send_kinds
            )
        else:
            state, carry, base = call(inner, outs, *args, pick, send_kinds)
        stacks, *later = call(
            functools.partial(outer_kernel, segment),
            sending,
            *came, *sent, kinds, meet, reach, send_kinds, base,
        )
    (out,) = call(
        last_kernel, [arr(256, 256)], *came, *sent, kinds, own_place, lift_two, ahead
    )
    return out.reshape(4, 64, ELEMENTS)


def solution(mesh):
    in_specs = (
        P(None, None, ("sec", "dom")),
        P(("sec", "dom")),
        P(("sec", "dom")),
        P(("sec", "dom")),
        P(None, ("sec", "dom")),
    )
    out_specs = P(None, None, ("sec", "dom"))
    return jax.shard_map(step, mesh=mesh, in_specs=in_specs, out_specs=out_specs, check_vma=False)
```

```python
import functools

import jax
import jax.numpy as jnp
import numpy as np
from jax import lax
from jax.experimental import pallas as pl
from jax.experimental.pallas import tpu as pltpu
from jax.sharding import PartitionSpec as P


FACE_CAP = 24
PIECES = 3
LANES = 128
ELEMENTS = 256
ROWS = 256
TRACE_ROWS = 48
LIFT = 3.0
TIME_STEP = 0.12
SEGMENT_CARRY = [
    0.0,
    -567301805773.0 / 1357537059087.0,
    -2404267990393.0 / 2016746695238.0,
    -3550918686646.0 / 2091501179385.0,
    -1275806237668.0 / 842570457699.0,
]
SEGMENT_WEIGHTS = [
    1432997174477.0 / 9575080441755.0,
    5161836677717.0 / 13612068292357.0,
    1720146321549.0 / 2090206949498.0,
    3134564353537.0 / 4481467310338.0,
    2277821191437.0 / 14882151754819.0,
]
BF = jnp.bfloat16
F32 = jnp.float32


def node_derivative():
    points = np.array([-1.0, -1.0 / np.sqrt(5.0), 1.0 / np.sqrt(5.0), 1.0])
    products = np.array(
        [np.prod([points[row] - points[col] for col in range(4) if col != row]) for row in range(4)]
    )
    matrix = np.zeros((4, 4))
    for row in range(4):
        for col in range(4):
            if row != col:
                matrix[row, col] = products[row] / (products[col] * (points[row] - points[col]))
        matrix[row, row] = -np.sum(matrix[row])
    return matrix


def along(matrix, direction):
    eye = np.eye(4)
    parts = [eye, eye, eye]
    parts[direction] = matrix
    return np.kron(np.kron(parts[0], parts[1]), parts[2])


def face_nodes(face):
    direction, side = divmod(face, 2)
    index = np.arange(64).reshape(4, 4, 4)
    return np.take(index, 3 * side, axis=direction).reshape(-1)


def interior_matrix():
    derivative = node_derivative()
    total = np.zeros((256, 256))
    for a in range(3):
        d = along(derivative, a)
        total[0:64, 64 * (a + 1) : 64 * (a + 2)] -= d
        total[64 * (a + 1) : 64 * (a + 2), 0:64] -= d
    for face in range(6):
        a, side = divmod(face, 2)
        sign = 2.0 * side - 1.0
        nodes = face_nodes(face)
        va = 64 * (a + 1) + nodes
        total[nodes, nodes] -= LIFT
        total[nodes, va] += LIFT * sign
        total[va, va] -= LIFT
        total[va, nodes] += LIFT * sign
        for b in range(3):
            if b != a:
                vb = 64 * (b + 1) + nodes
                total[vb, vb] -= LIFT
    return total


def trace_matrix():
    total = np.zeros((6 * TRACE_ROWS, 256))
    for face in range(6):
        a, side = divmod(face, 2)
        sign = 2.0 * side - 1.0
        nodes = face_nodes(face)
        rows = TRACE_ROWS * face + np.arange(16)
        total[rows, nodes] = 1.0
        total[rows, 64 * (a + 1) + nodes] = sign
        for number, b in enumerate([b for b in range(3) if b != a]):
            total[rows + 16 * (number + 1), 64 * (b + 1) + nodes] = 1.0
    return total


def lift_matrix():
    total = np.zeros((256, 6 * TRACE_ROWS))
    for face in range(6):
        a, side = divmod(face, 2)
        sign = 2.0 * side - 1.0
        nodes = face_nodes(face)
        cols = TRACE_ROWS * face + np.arange(16)
        total[nodes, cols] = 1.0
        total[64 * (a + 1) + nodes, cols] = -sign
        for number, b in enumerate([b for b in range(3) if b != a]):
            total[64 * (b + 1) + nodes, cols + 16 * (number + 1)] = 1.0
    return total


def two_terms(matrix):
    high = matrix.astype(np.float32).astype(BF)
    low = (matrix - high.astype(np.float64)).astype(np.float32).astype(BF)
    return high, low


def mm(a, b):
    return lax.dot_general(a, b, (((1,), (0,)), ((), ())), preferred_element_type=F32)


def mm_nt(a, b):
    return lax.dot_general(a, b, (((1,), (1,)), ((), ())), preferred_element_type=F32)


def split(x):
    high = x.astype(BF)
    return high, (x - high.astype(F32)).astype(BF)


def one_hot(mask):
    return jnp.where(mask, 1.0, 0.0).astype(BF)


def lane_iota(shape):
    return lax.broadcasted_iota(jnp.int32, shape, 1)


def row_iota(shape):
    return lax.broadcasted_iota(jnp.int32, shape, 0)


def picked_traces(state, pick, kinds, trace):
    high, low = split(state)
    chosen = jnp.concatenate([mm(high, pick).astype(BF), mm(low, pick).astype(BF)], axis=1)
    shown = mm(trace, chosen)
    return of_kind(shown[:, :256] + shown[:, 256:], kinds)


def of_kind(shown, kinds):
    total = jnp.zeros((TRACE_ROWS, 256), F32)
    for face in range(6):
        part = shown[TRACE_ROWS * face : TRACE_ROWS * (face + 1)]
        total = total + jnp.where(kinds[face : face + 1] > 0, part, 0.0)
    return total


def by_kind(came, sent, kinds):
    far = lane_iota((TRACE_ROWS, LANES)) < PIECES * FACE_CAP
    from_left, from_right = sides(*came)
    own_left, own_right = sides(*sent)
    got = jnp.concatenate(
        [jnp.where(far, from_right, own_left), jnp.where(far, from_left, own_right)], axis=1
    )
    masked = jnp.concatenate(
        [jnp.where(kinds[face : face + 1] > 0, got, 0.0) for face in range(6)], axis=0
    )
    return jnp.concatenate(split(masked), axis=0)


def far_rates(stacks, place, lift_two):
    return mm(lift_two, mm(stacks, place).astype(BF))


def sides(first, second):
    odd = ((lax.axis_index("dom") >> 1) & 1) == 1
    return jnp.where(odd, second, first), jnp.where(odd, first, second)


def core_number():
    return lax.axis_index("dom") & 1


def chip_halves(mine, other):
    first = core_number() == 0
    return jnp.where(first, mine, other), jnp.where(first, other, mine)


def difference_along(stride):
    row, col = row_iota((64, 64)), lane_iota((64, 64))
    at, step = (row // stride) & 3, ((col // stride) & 3) - ((row // stride) & 3)
    inner = jnp.where(step == 1, 0.5, jnp.where(step == -1, -0.5, 0.0))
    lower = jnp.where(step == 1, 1.0, jnp.where(step == 0, -1.0, 0.0))
    upper = jnp.where(step == 0, 1.0, jnp.where(step == -1, -1.0, 0.0))
    value = jnp.where(at == 0, lower, jnp.where(at == 3, upper, inner))
    return jnp.where(col - row == step * stride, value, 0.0).astype(BF)


def lamb_kernel(packed, lamb_out):
    slopes = jnp.concatenate([difference_along(stride) for stride in (16, 4, 1)], axis=0)
    v = [packed[64 * a : 64 * (a + 1)] for a in range(3)]
    high, low = split(jnp.concatenate(v, axis=1))
    found = mm(slopes, high) + mm(slopes, low)

    def slope(component, direction):
        return found[64 * direction : 64 * direction + 64, 256 * component : 256 * component + 256]

    w = [
        slope(2, 1) - slope(1, 2),
        slope(0, 2) - slope(2, 0),
        slope(1, 0) - slope(0, 1),
    ]
    rho = packed[192:256]
    lamb_out[0:64] = rho * (w[1] * v[2] - w[2] * v[1])
    lamb_out[64:128] = rho * (w[2] * v[0] - w[0] * v[2])
    lamb_out[128:192] = rho * (w[0] * v[1] - w[1] * v[0])


def group_of(device, offset):
    return 8 * device + {0: 0, -2: 1, -1: 2, 1: 3, 2: 4}[offset]


def start_of(count, device, offset):
    total = jnp.zeros((1, 1), F32)
    for number in (0, -2, -1, 1, 2):
        if number == offset:
            return total
        at = group_of(device, number)
        total = total + count[at : at + 1]


def target_of(members, rank, device, moves):
    total = jnp.full((1, 256), -1.0, F32)
    for offset, base in moves:
        at = group_of(device, offset)
        total = total + members[at : at + 1] * (rank[at : at + 1] + (base + 1.0))
    return total


def depart_kernel(mine, other, first_out, second_out, select_out, ranks_out):
    low, high = chip_halves(mine[...], other[...])
    first = (lax.axis_index("dom") & -2).astype(F32)
    spread = one_hot((lane_iota((64, 256)) >> 2) == row_iota((64, 256)))
    before = one_hot(row_iota((256, 256)) < lane_iota((256, 256)))
    row8 = row_iota((8, 256))
    wanted = jnp.where(row8 == 0, 0, jnp.where(row8 < 3, row8 - 3, row8 - 2)).astype(F32)
    members = []
    for number, half in enumerate((low, high)):
        owner = half[263:264, 0:64] - (first + number)
        owner = jnp.clip(jnp.broadcast_to(owner, (8, 64)), -8.0, 8.0).astype(BF)
        member = (mm(owner, spread) == wanted) & (row8 < 5)
        members.append(jnp.where(member, 1.0, 0.0))
    members = jnp.concatenate(members, axis=0)
    rank = mm(members.astype(BF), before)
    ranks_out[0:16] = members
    ranks_out[16:32] = rank
    low_target = target_of(members, rank, 0, ((-2, 0.0), (-1, 16.0), (2, 48.0)))
    high_target = target_of(members, rank, 1, ((-2, 32.0), (1, 64.0), (2, 80.0)))
    number = row_iota((96, 256)).astype(F32)
    select = jnp.concatenate([one_hot(low_target == number), one_hot(high_target == number)], axis=1)
    select_out[...] = select
    cells = jnp.concatenate([low[0:256], high[0:256]], axis=1)
    cells_high, cells_low = split(cells)
    sent = mm_nt(select, cells_high) + mm_nt(select, cells_low)
    first_out[...], second_out[...] = sides(sent[0:48], sent[48:96])


def places_kernel(
    mine, other, ranks, trace,
    kept_out, keep_out, arrive_out, pick_out, send_kinds_out, arrive_pick_out, base_out,
):
    low, high = chip_halves(mine[...], other[...])
    members, rank = ranks[0:16], ranks[16:32]
    count = jnp.sum(members, axis=1, keepdims=True)
    low_place = target_of(members, rank, 0, ((0, 0.0), (1, 256.0 + start_of(count, 1, -1))))
    high_place = target_of(members, rank, 1, ((0, 256.0), (-1, start_of(count, 0, 1))))
    number = row_iota((512, 256)).astype(F32)
    keep = jnp.concatenate([one_hot(low_place == number), one_hot(high_place == number)], axis=1)
    keep_out[...] = keep
    column = lane_iota((16, 512)).astype(F32)
    number = row_iota((16, 512)).astype(F32)
    blocks = []
    for device, offset in ((0, -2), (0, -1), (1, -2), (0, 2), (1, 1), (1, 2)):
        at = group_of(device, offset)
        begin = start_of(count, device, offset) + 256.0 * device
        blocks.append(one_hot((column - begin == number) & (number < count[at : at + 1])))
    arrive = jnp.concatenate(blocks, axis=0)
    arrive_out[...] = arrive
    cells_high, cells_low = split(jnp.concatenate([low[0:256], high[0:256]], axis=1))
    kept = mm_nt(cells_high, keep) + mm_nt(cells_low, keep)
    kept_out[...] = kept
    lane = lane_iota((8, LANES))
    lists = [jnp.broadcast_to(half[263:264, 128:256], (8, LANES)) for half in (low, high)]
    left = jnp.where(lane < 48, lists[0], pltpu.roll(lists[1], 48, 1))
    right = jnp.where(
        lane < 24,
        pltpu.roll(lists[0], LANES - 72, 1),
        jnp.where(lane < 72, pltpu.roll(lists[1], LANES - 24, 1), pltpu.roll(lists[0], 24, 1)),
    )
    names = jnp.concatenate(
        [jnp.where(lane < 96, left, -1.0), jnp.where(lane < 96, right, -1.0)], axis=1
    ).astype(jnp.int32)
    wide = lane_iota((8, 256))
    second = ((wide >= 48) & (wide < 128)) | ((wide >= 152) & (wide < 200))
    column = jnp.where(names < 0, -1, (names & 255) + jnp.where(second, 256, 0))
    pick = one_hot(column[0:1] == row_iota((512, 256)))
    pick_out[...] = pick
    send_kinds = jnp.where((names >> 8) == row_iota((8, 256)), 1.0, 0.0)
    send_kinds_out[...] = send_kinds
    arrive_pick_out[...] = mm(arrive, pick).astype(BF)
    base_out[...] = picked_traces(kept, pick, send_kinds, trace[...])


def faces_kernel(mine, other, pick, local_out, place_out, own_place_out, kinds_out, meet_out):
    row = row_iota((256, 256))
    ones = jnp.ones((8, 256), BF)
    kinds = [jnp.zeros((1, 256), F32)] * 6
    places = []
    for device, half in enumerate(chip_halves(mine[256:264], other[256:264])):
        place = jnp.zeros((256, 256), F32)
        for face in range(6):
            where = half[face : face + 1].astype(jnp.int32)
            local_out[6 * device + face] = one_hot(where - ELEMENTS * (face ^ 1) == row)
            n = where - 6 * ELEMENTS
            if device == 0:
                entry = jnp.where(n < 48, n + 128, jnp.where(n < 72, n + 24, n - 72))
            else:
                entry = jnp.where(n < 48, n + 176, n - 24)
            hit = jnp.where(jnp.where(n < 0, -1, entry) == row, 1.0, 0.0)
            place = place + hit
            kinds[face] = kinds[face] + mm_nt(ones, hit.astype(BF))[0:1]
        places.append(place)
    own_place_out[...] = jnp.where(core_number() == 0, places[0], places[1]).astype(BF)
    place = jnp.concatenate(places, axis=1).astype(BF)
    place_out[...] = place
    kinds_out[...] = jnp.concatenate(kinds + [jnp.zeros((2, 256), F32)], axis=0)
    meet_out[...] = mm(place, pick[...]).astype(BF)


def force_kernel(first, second, third, packed, out):
    lamb = first[...] + second[...] + third[...]
    high, low = split(lamb)
    source = one_hot(packed[262:263].astype(jnp.int32) == row_iota((256, 256)))
    out[...] = mm(high, source) + mm(low, source)


def came_columns(first, second):
    return split(jnp.transpose(jnp.concatenate(sides(first, second), axis=0)))


def leave_kernel(
    first, second, base, arrive_pick, send_kinds, trace, force_mine, force_other, select,
    wide_first, wide_second, own_first, own_second,
):
    chosen = [mm(term, arrive_pick[...]).astype(BF) for term in came_columns(first[...], second[...])]
    shown = mm(trace[...], jnp.concatenate(chosen, axis=1))
    sent = base[...] + of_kind(shown[:, :256] + shown[:, 256:], send_kinds[...])
    own = sides(sent[:, :LANES], sent[:, LANES:])
    force = jnp.concatenate(chip_halves(force_mine[...], force_other[...]), axis=1)
    high, low = split(force)
    moved = mm_nt(select[...], high) + mm_nt(select[...], low)
    pieces = sides(moved[0:48], moved[48:96])
    for wide, piece, part in zip((wide_first, wide_second), pieces, own):
        wide[:, 0:192] = piece
        wide[:, 192:256] = jnp.zeros((48, 64), F32)
        wide[:, 256:384] = part
    own_first[...], own_second[...] = own


def near_rates(state, near, interior, trace, lift_two):
    high, low = split(state)
    rates = mm(interior, jnp.concatenate([high, low, high], axis=0))
    shown = mm(trace, jnp.concatenate([high, low], axis=1))
    shown_high, shown_low = split(shown[:, 0:512] + shown[:, 512:1024])
    faces = []
    for device in range(2):
        columns = slice(256 * device, 256 * (device + 1))
        outside_high, outside_low = [], []
        for face in range(6):
            rows = slice(TRACE_ROWS * (face ^ 1), TRACE_ROWS * (face ^ 1) + TRACE_ROWS)
            stacked = jnp.concatenate([shown_high[rows, columns], shown_low[rows, columns]], axis=0)
            found = mm(stacked, near[6 * device + face]).astype(BF)
            outside_high.append(found[:TRACE_ROWS])
            outside_low.append(found[TRACE_ROWS:])
        faces.append(jnp.concatenate(outside_high + outside_low, axis=0))
    return rates + LIFT * mm(lift_two, jnp.concatenate(faces, axis=1))


def weight_of(segment):
    acoustic = lax.axis_index("sec") > 0
    return jnp.where(acoustic, F32(SEGMENT_WEIGHTS[segment]), F32(0.0))


def first_inner_kernel(
    first, second, kept, arrive, force_mine, force_other, keep, near, interior, trace, lift_two,
    pick, send_kinds, state_out, carry_out, force_out, base_out,
):
    high, low = came_columns(first[...], second[...])
    state = kept[...] + (mm(high, arrive[...]) + mm(low, arrive[...]))
    state_out[...] = state
    high, low = split(jnp.concatenate(chip_halves(force_mine[...], force_other[...]), axis=1))
    force = mm_nt(high, keep[...]) + mm_nt(low, keep[...])
    force_out[...] = force
    own = TIME_STEP * near_rates(state, near, interior[...], trace[...], lift_two[...])
    own = jnp.concatenate([own[0:64], own[64:256] + TIME_STEP * force], axis=0)
    carry_out[...] = own
    ahead = state + weight_of(0) * own
    base_out[...] = picked_traces(ahead, pick[...], send_kinds[...], trace[...])


def first_outer_kernel(
    first, second, sent_first, sent_second, kinds, meet, reach, send_kinds, base, trace, arrive_pick,
    stacks_out, first_out, second_out,
):
    stacks = by_kind(
        (first[:, 256:384], second[:, 256:384]), (sent_first[...], sent_second[...]), kinds[...]
    )
    stacks_out[...] = stacks
    shown = LIFT * mm(reach[...], mm(stacks, meet[...]).astype(BF))
    chosen = [
        jnp.concatenate([jnp.zeros((64, 256), BF), mm(term[0:192], arrive_pick[...]).astype(BF)], axis=0)
        for term in came_columns(first[:, 0:256], second[:, 0:256])
    ]
    pushed = mm(trace[...], jnp.concatenate(chosen, axis=1))
    shown = shown + (pushed[:, :256] + pushed[:, 256:])
    sent = base[...] + (weight_of(0) * F32(TIME_STEP)) * of_kind(shown, send_kinds[...])
    first_out[...], second_out[...] = sides(sent[:, :LANES], sent[:, LANES:])


def inner_kernel(segment, state, carry, force, stacks, place, near, interior, trace, lift_two, *refs):
    rates = far_rates(stacks[...], place[...], lift_two[...])
    carry_now = carry[...] + (LIFT * TIME_STEP) * rates
    force = force[...]
    if segment == 1:
        (first, second, arrive), refs = refs[:3], refs[3:]
        high, low = came_columns(first[:, 0:256], second[:, 0:256])
        came = mm(high[0:192], arrive[...]) + mm(low[0:192], arrive[...])
        carry_now = jnp.concatenate([carry_now[0:64], carry_now[64:256] + TIME_STEP * came], axis=0)
        force = force + came
    state_now = state[...] + weight_of(segment - 1) * carry_now
    rates = near_rates(state_now, near, interior[...], trace[...], lift_two[...])
    own = SEGMENT_CARRY[segment] * carry_now + TIME_STEP * rates
    own = jnp.concatenate([own[0:64], own[64:256] + TIME_STEP * force], axis=0)
    ahead = state_now + weight_of(segment) * own
    if segment == 4:
        refs[0][...] = jnp.where(core_number() == 0, ahead[:, 0:256], ahead[:, 256:512])
        return
    (pick, send_kinds, state_out, carry_out, base_out), refs = refs[:5], refs[5:]
    state_out[...] = state_now
    carry_out[...] = own
    base_out[...] = picked_traces(ahead, pick[...], send_kinds[...], trace[...])
    if segment == 1:
        refs[0][...] = force


def outer_kernel(
    segment, first, second, sent_first, sent_second, kinds, meet, reach, send_kinds, base,
    stacks_out, first_out, second_out,
):
    stacks = by_kind((first[...], second[...]), (sent_first[...], sent_second[...]), kinds[...])
    stacks_out[...] = stacks
    shown = mm(reach[...], mm(stacks, meet[...]).astype(BF))
    sent = base[...] + (weight_of(segment) * F32(LIFT * TIME_STEP)) * of_kind(shown, send_kinds[...])
    first_out[...], second_out[...] = sides(sent[:, :LANES], sent[:, LANES:])


def last_kernel(
    first, second, sent_first, sent_second, kinds, own_place, lift_two, ahead, out, held, done
):
    stacks = by_kind((first[...], second[...]), (sent_first[...], sent_second[...]), kinds[...])
    outside = mm(stacks, own_place[...]).astype(BF)
    scale = weight_of(4) * F32(LIFT * TIME_STEP)
    copies = []
    for number, rows in enumerate((slice(0, 128), slice(128, 256))):
        held[rows] = ahead[rows] + scale * mm(lift_two[rows], outside)
        copies.append(pltpu.make_async_copy(held.at[rows], out.at[rows], done.at[number]))
        copies[-1].start()
    for copy in copies:
        copy.wait()


def call(kernel, outs, *args, flops=1 << 20, far=False, scratch=()):
    vmem = pl.BlockSpec(memory_space=pltpu.VMEM)
    size = sum(int(np.prod(a.shape)) * a.dtype.itemsize for a in (*args, *outs))
    return pl.pallas_call(
        kernel,
        out_shape=list(outs),
        in_specs=[vmem] * len(args),
        out_specs=[pl.BlockSpec(memory_space=pl.ANY) if far else vmem] * len(outs),
        scratch_shapes=list(scratch),
        compiler_params=pltpu.CompilerParams(vmem_limit_bytes=32 << 20),
        cost_estimate=pl.CostEstimate(flops=flops, bytes_accessed=size, transcendentals=0),
    )(*args)


def arr(*shape, dtype=F32):
    return jax.ShapeDtypeStruct(shape, dtype)


def trade(first, second, sections):
    count = lax.axis_size("dom")
    came = []
    for value, odd in ((first, 1), (second, 0)):
        pairs = []
        for section in sections:
            for dom in range(count - 2):
                if (dom >> 1) & 1 == odd:
                    low = section * count + dom
                    pairs += [(low, low + 2), (low + 2, low)]
        came.append(lax.ppermute(value, ("sec", "dom"), pairs))
    return came


def swap(value):
    return lax.ppermute(value, "dom", [(at, at ^ 1) for at in range(lax.axis_size("dom"))])


def step(fields, source_map, new_owner, send_list, face_slot):
    cells = fields.reshape(ROWS, ELEMENTS)
    high, low = two_terms(interior_matrix())
    interior = jnp.asarray(np.concatenate([high, high, low], axis=1))
    trace = jnp.asarray(trace_matrix().astype(BF))
    lift_two = jnp.asarray(np.concatenate([lift_matrix()] * 2, axis=1).astype(BF))
    reach = jnp.asarray(np.concatenate([trace_matrix() @ lift_matrix()] * 2, axis=1).astype(BF))
    every = range(lax.axis_size("sec"))
    acoustic = every[1:]
    piece, whole = arr(TRACE_ROWS, LANES), arr(256, 512)

    names = jnp.zeros((264, 256), jnp.int32)
    for part, row, lane in (
        (face_slot, 256, 0),
        (source_map.reshape(1, 256), 262, 0),
        (new_owner.reshape(1, 64), 263, 0),
        (send_list.reshape(1, 96), 263, 128),
    ):
        rows, lanes = part.shape
        edges = ((row, 264 - row - rows, 0), (lane, 256 - lane - lanes, 0))
        names = names + lax.pad(part, jnp.int32(0), edges)
    packed = names.astype(F32) + lax.pad(cells, F32(0.0), ((0, 8, 0), (0, 0, 0)))
    (lamb,) = call(lamb_kernel, [arr(192, 256)], packed)
    lamb_parts = []
    for section in (1, 2, 3):
        lamb_parts.append(lax.ppermute(lamb, "sec", [(0, section)]))
    other = swap(packed)
    *leaving, select, ranks = call(
        depart_kernel,
        [arr(48, 256), arr(48, 256), arr(96, 512, dtype=BF), arr(32, 256)],
        packed,
        other,
    )
    moved = trade(*leaving, every)
    (force_mine,) = call(force_kernel, [arr(192, 256)], *lamb_parts, packed)
    force_other = swap(force_mine)
    kept, keep, arrive, pick, send_kinds, arrive_pick, base = call(
        places_kernel,
        [
            whole,
            arr(512, 512, dtype=BF),
            arr(96, 512, dtype=BF),
            arr(512, 256, dtype=BF),
            arr(8, 256),
            arr(96, 256, dtype=BF),
            arr(TRACE_ROWS, 256),
        ],
        packed,
        other,
        ranks,
        trace,
    )
    *wide, own_first, own_second = call(
        leave_kernel,
        [arr(48, 384), arr(48, 384), piece, piece],
        *moved, base, arrive_pick, send_kinds, trace, force_mine, force_other, select,
    )
    sent = [own_first, own_second]
    came = trade(*wide, acoustic)
    near, place, own_place, kinds, meet = call(
        faces_kernel,
        [
            arr(12, 256, 256, dtype=BF),
            arr(256, 512, dtype=BF),
            arr(256, 256, dtype=BF),
            arr(8, 256),
            arr(256, 256, dtype=BF),
        ],
        packed,
        other,
        pick,
    )
    state, carry, force, base = call(
        first_inner_kernel,
        [whole, whole, arr(192, 512), arr(TRACE_ROWS, 256)],
        *moved, kept, arrive, force_mine, force_other, keep, near, interior, trace, lift_two,
        pick, send_kinds,
    )
    sending = [arr(12 * TRACE_ROWS, 256, dtype=BF), piece, piece]
    stacks, *later = call(
        first_outer_kernel,
        sending,
        *came, *sent, kinds, meet, reach, send_kinds, base, trace, arrive_pick,
    )
    extra = [*came, arrive]
    for segment in range(1, 5):
        sent, came = later, trade(*later, acoustic)
        inner = functools.partial(inner_kernel, segment)
        args = [state, carry, force, stacks, place, near, interior, trace, lift_two]
        if segment == 4:
            (ahead,) = call(inner, [arr(256, 256)], *args)
            break
        outs = [whole, whole, arr(TRACE_ROWS, 256)]
        if segment == 1:
            state, carry, base, force = call(
                inner, [*outs, arr(192, 512)], *args, *extra, pick, send_kinds
            )
        else:
            state, carry, base = call(inner, outs, *args, pick, send_kinds)
        stacks, *later = call(
            functools.partial(outer_kernel, segment),
            sending,
            *came, *sent, kinds, meet, reach, send_kinds, base,
        )
    (out,) = call(
        last_kernel,
        [arr(256, 256)],
        *came, *sent, kinds, own_place, lift_two, ahead,
        far=True,
        scratch=(pltpu.VMEM((256, 256), F32), pltpu.SemaphoreType.DMA((2,))),
    )
    return out.reshape(4, 64, ELEMENTS)


def solution(mesh):
    in_specs = (
        P(None, None, ("sec", "dom")),
        P(("sec", "dom")),
        P(("sec", "dom")),
        P(("sec", "dom")),
        P(None, ("sec", "dom")),
    )
    out_specs = P(None, None, ("sec", "dom"))
    return jax.shard_map(step, mesh=mesh, in_specs=in_specs, out_specs=out_specs, check_vma=False)
```

```python
import functools

import jax
import jax.numpy as jnp
import numpy as np
from jax import lax
from jax.experimental import pallas as pl
from jax.experimental.pallas import tpu as pltpu
from jax.sharding import PartitionSpec as P


FACE_CAP = 24
PIECES = 3
LANES = 128
ELEMENTS = 256
ROWS = 256
TRACE_ROWS = 48
LIFT = 3.0
TIME_STEP = 0.12
SEGMENT_CARRY = [
    0.0,
    -567301805773.0 / 1357537059087.0,
    -2404267990393.0 / 2016746695238.0,
    -3550918686646.0 / 2091501179385.0,
    -1275806237668.0 / 842570457699.0,
]
SEGMENT_WEIGHTS = [
    1432997174477.0 / 9575080441755.0,
    5161836677717.0 / 13612068292357.0,
    1720146321549.0 / 2090206949498.0,
    3134564353537.0 / 4481467310338.0,
    2277821191437.0 / 14882151754819.0,
]
BF = jnp.bfloat16
F32 = jnp.float32


def node_derivative():
    points = np.array([-1.0, -1.0 / np.sqrt(5.0), 1.0 / np.sqrt(5.0), 1.0])
    products = np.array(
        [np.prod([points[row] - points[col] for col in range(4) if col != row]) for row in range(4)]
    )
    matrix = np.zeros((4, 4))
    for row in range(4):
        for col in range(4):
            if row != col:
                matrix[row, col] = products[row] / (products[col] * (points[row] - points[col]))
        matrix[row, row] = -np.sum(matrix[row])
    return matrix


def along(matrix, direction):
    eye = np.eye(4)
    parts = [eye, eye, eye]
    parts[direction] = matrix
    return np.kron(np.kron(parts[0], parts[1]), parts[2])


def face_nodes(face):
    direction, side = divmod(face, 2)
    index = np.arange(64).reshape(4, 4, 4)
    return np.take(index, 3 * side, axis=direction).reshape(-1)


def interior_matrix():
    derivative = node_derivative()
    total = np.zeros((256, 256))
    for a in range(3):
        d = along(derivative, a)
        total[0:64, 64 * (a + 1) : 64 * (a + 2)] -= d
        total[64 * (a + 1) : 64 * (a + 2), 0:64] -= d
    for face in range(6):
        a, side = divmod(face, 2)
        sign = 2.0 * side - 1.0
        nodes = face_nodes(face)
        va = 64 * (a + 1) + nodes
        total[nodes, nodes] -= LIFT
        total[nodes, va] += LIFT * sign
        total[va, va] -= LIFT
        total[va, nodes] += LIFT * sign
        for b in range(3):
            if b != a:
                vb = 64 * (b + 1) + nodes
                total[vb, vb] -= LIFT
    return total


def trace_matrix():
    total = np.zeros((6 * TRACE_ROWS, 256))
    for face in range(6):
        a, side = divmod(face, 2)
        sign = 2.0 * side - 1.0
        nodes = face_nodes(face)
        rows = TRACE_ROWS * face + np.arange(16)
        total[rows, nodes] = 1.0
        total[rows, 64 * (a + 1) + nodes] = sign
        for number, b in enumerate([b for b in range(3) if b != a]):
            total[rows + 16 * (number + 1), 64 * (b + 1) + nodes] = 1.0
    return total


def lift_matrix():
    total = np.zeros((256, 6 * TRACE_ROWS))
    for face in range(6):
        a, side = divmod(face, 2)
        sign = 2.0 * side - 1.0
        nodes = face_nodes(face)
        cols = TRACE_ROWS * face + np.arange(16)
        total[nodes, cols] = 1.0
        total[64 * (a + 1) + nodes, cols] = -sign
        for number, b in enumerate([b for b in range(3) if b != a]):
            total[64 * (b + 1) + nodes, cols + 16 * (number + 1)] = 1.0
    return total


def two_terms(matrix):
    high = matrix.astype(np.float32).astype(BF)
    low = (matrix - high.astype(np.float64)).astype(np.float32).astype(BF)
    return high, low


def mm(a, b):
    return lax.dot_general(a, b, (((1,), (0,)), ((), ())), preferred_element_type=F32)


def mm_nt(a, b):
    return lax.dot_general(a, b, (((1,), (1,)), ((), ())), preferred_element_type=F32)


def split(x):
    high = x.astype(BF)
    return high, (x - high.astype(F32)).astype(BF)


def one_hot(mask):
    return jnp.where(mask, 1.0, 0.0).astype(BF)


def lane_iota(shape):
    return lax.broadcasted_iota(jnp.int32, shape, 1)


def row_iota(shape):
    return lax.broadcasted_iota(jnp.int32, shape, 0)


def picked_traces(state, pick, kinds, trace):
    high, low = split(state)
    chosen = jnp.concatenate([mm(high, pick).astype(BF), mm(low, pick).astype(BF)], axis=1)
    shown = mm(trace, chosen)
    return of_kind(shown[:, :256] + shown[:, 256:], kinds)


def of_kind(shown, kinds):
    total = jnp.zeros((TRACE_ROWS, 256), F32)
    for face in range(6):
        part = shown[TRACE_ROWS * face : TRACE_ROWS * (face + 1)]
        total = total + jnp.where(kinds[face : face + 1] > 0, part, 0.0)
    return total


def by_kind(came, sent, kinds):
    far = lane_iota((TRACE_ROWS, LANES)) < PIECES * FACE_CAP
    from_left, from_right = sides(*came)
    own_left, own_right = sides(*sent)
    got = jnp.concatenate(
        [jnp.where(far, from_right, own_left), jnp.where(far, from_left, own_right)], axis=1
    )
    masked = jnp.concatenate(
        [jnp.where(kinds[face : face + 1] > 0, got, 0.0) for face in range(6)], axis=0
    )
    return jnp.concatenate(split(masked), axis=0)


def far_rates(stacks, place, lift_two):
    return mm(lift_two, mm(stacks, place).astype(BF))


def sides(first, second):
    odd = ((lax.axis_index("dom") >> 1) & 1) == 1
    return jnp.where(odd, second, first), jnp.where(odd, first, second)


def core_number():
    return lax.axis_index("dom") & 1


def chip_halves(mine, other):
    first = core_number() == 0
    return jnp.where(first, mine, other), jnp.where(first, other, mine)


def difference_along(stride):
    row, col = row_iota((64, 64)), lane_iota((64, 64))
    at, step = (row // stride) & 3, ((col // stride) & 3) - ((row // stride) & 3)
    inner = jnp.where(step == 1, 0.5, jnp.where(step == -1, -0.5, 0.0))
    lower = jnp.where(step == 1, 1.0, jnp.where(step == 0, -1.0, 0.0))
    upper = jnp.where(step == 0, 1.0, jnp.where(step == -1, -1.0, 0.0))
    value = jnp.where(at == 0, lower, jnp.where(at == 3, upper, inner))
    return jnp.where(col - row == step * stride, value, 0.0).astype(BF)


def lamb_kernel(packed, lamb_out):
    slopes = jnp.concatenate([difference_along(stride) for stride in (16, 4, 1)], axis=0)
    v = [packed[64 * a : 64 * (a + 1)] for a in range(3)]
    high, low = split(jnp.concatenate(v, axis=1))
    found = mm(slopes, high) + mm(slopes, low)

    def slope(component, direction):
        return found[64 * direction : 64 * direction + 64, 256 * component : 256 * component + 256]

    w = [
        slope(2, 1) - slope(1, 2),
        slope(0, 2) - slope(2, 0),
        slope(1, 0) - slope(0, 1),
    ]
    rho = packed[192:256]
    lamb_out[0:64] = rho * (w[1] * v[2] - w[2] * v[1])
    lamb_out[64:128] = rho * (w[2] * v[0] - w[0] * v[2])
    lamb_out[128:192] = rho * (w[0] * v[1] - w[1] * v[0])


def group_of(device, offset):
    return 8 * device + {0: 0, -2: 1, -1: 2, 1: 3, 2: 4}[offset]


def start_of(count, device, offset):
    total = jnp.zeros((1, 1), F32)
    for number in (0, -2, -1, 1, 2):
        if number == offset:
            return total
        at = group_of(device, number)
        total = total + count[at : at + 1]


def target_of(members, rank, device, moves):
    total = jnp.full((1, 256), -1.0, F32)
    for offset, base in moves:
        at = group_of(device, offset)
        total = total + members[at : at + 1] * (rank[at : at + 1] + (base + 1.0))
    return total


def depart_kernel(mine, other, other_flow, first_out, second_out, select_out, ranks_out):
    low, high = chip_halves(mine[...], other[...] + other_flow[...])
    first = (lax.axis_index("dom") & -2).astype(F32)
    spread = one_hot((lane_iota((64, 256)) >> 2) == row_iota((64, 256)))
    before = one_hot(row_iota((256, 256)) < lane_iota((256, 256)))
    row8 = row_iota((8, 256))
    wanted = jnp.where(row8 == 0, 0, jnp.where(row8 < 3, row8 - 3, row8 - 2)).astype(F32)
    members = []
    for number, half in enumerate((low, high)):
        owner = half[263:264, 0:64] - (first + number)
        owner = jnp.clip(jnp.broadcast_to(owner, (8, 64)), -8.0, 8.0).astype(BF)
        member = (mm(owner, spread) == wanted) & (row8 < 5)
        members.append(jnp.where(member, 1.0, 0.0))
    members = jnp.concatenate(members, axis=0)
    rank = mm(members.astype(BF), before)
    ranks_out[0:16] = members
    ranks_out[16:32] = rank
    low_target = target_of(members, rank, 0, ((-2, 0.0), (-1, 16.0), (2, 48.0)))
    high_target = target_of(members, rank, 1, ((-2, 32.0), (1, 64.0), (2, 80.0)))
    number = row_iota((96, 256)).astype(F32)
    select = jnp.concatenate([one_hot(low_target == number), one_hot(high_target == number)], axis=1)
    select_out[...] = select
    cells = jnp.concatenate([low[0:256], high[0:256]], axis=1)
    cells_high, cells_low = split(cells)
    sent = mm_nt(select, cells_high) + mm_nt(select, cells_low)
    first_out[...], second_out[...] = sides(sent[0:48], sent[48:96])


def places_kernel(
    mine, other, other_flow, ranks, trace,
    kept_out, keep_out, arrive_out, pick_out, send_kinds_out, arrive_pick_out, base_out,
):
    low, high = chip_halves(mine[...], other[...] + other_flow[...])
    members, rank = ranks[0:16], ranks[16:32]
    count = jnp.sum(members, axis=1, keepdims=True)
    low_place = target_of(members, rank, 0, ((0, 0.0), (1, 256.0 + start_of(count, 1, -1))))
    high_place = target_of(members, rank, 1, ((0, 256.0), (-1, start_of(count, 0, 1))))
    number = row_iota((512, 256)).astype(F32)
    keep = jnp.concatenate([one_hot(low_place == number), one_hot(high_place == number)], axis=1)
    keep_out[...] = keep
    column = lane_iota((16, 512)).astype(F32)
    number = row_iota((16, 512)).astype(F32)
    blocks = []
    for device, offset in ((0, -2), (0, -1), (1, -2), (0, 2), (1, 1), (1, 2)):
        at = group_of(device, offset)
        begin = start_of(count, device, offset) + 256.0 * device
        blocks.append(one_hot((column - begin == number) & (number < count[at : at + 1])))
    arrive = jnp.concatenate(blocks, axis=0)
    arrive_out[...] = arrive
    cells_high, cells_low = split(jnp.concatenate([low[0:256], high[0:256]], axis=1))
    kept = mm_nt(cells_high, keep) + mm_nt(cells_low, keep)
    kept_out[...] = kept
    lane = lane_iota((8, LANES))
    lists = [jnp.broadcast_to(half[263:264, 128:256], (8, LANES)) for half in (low, high)]
    left = jnp.where(lane < 48, lists[0], pltpu.roll(lists[1], 48, 1))
    right = jnp.where(
        lane < 24,
        pltpu.roll(lists[0], LANES - 72, 1),
        jnp.where(lane < 72, pltpu.roll(lists[1], LANES - 24, 1), pltpu.roll(lists[0], 24, 1)),
    )
    names = jnp.concatenate(
        [jnp.where(lane < 96, left, -1.0), jnp.where(lane < 96, right, -1.0)], axis=1
    ).astype(jnp.int32)
    wide = lane_iota((8, 256))
    second = ((wide >= 48) & (wide < 128)) | ((wide >= 152) & (wide < 200))
    column = jnp.where(names < 0, -1, (names & 255) + jnp.where(second, 256, 0))
    pick = one_hot(column[0:1] == row_iota((512, 256)))
    pick_out[...] = pick
    send_kinds = jnp.where((names >> 8) == row_iota((8, 256)), 1.0, 0.0)
    send_kinds_out[...] = send_kinds
    arrive_pick_out[...] = mm(arrive, pick).astype(BF)
    base_out[...] = picked_traces(kept, pick, send_kinds, trace[...])


def faces_kernel(mine, other, other_flow, pick, local_out, place_out, own_place_out, kinds_out, meet_out):
    row = row_iota((256, 256))
    ones = jnp.ones((8, 256), BF)
    kinds = [jnp.zeros((1, 256), F32)] * 6
    places = []
    for device, half in enumerate(chip_halves(mine[256:264], other[256:264] + other_flow[256:264])):
        place = jnp.zeros((256, 256), F32)
        for face in range(6):
            where = half[face : face + 1].astype(jnp.int32)
            local_out[6 * device + face] = one_hot(where - ELEMENTS * (face ^ 1) == row)
            n = where - 6 * ELEMENTS
            if device == 0:
                entry = jnp.where(n < 48, n + 128, jnp.where(n < 72, n + 24, n - 72))
            else:
                entry = jnp.where(n < 48, n + 176, n - 24)
            hit = jnp.where(jnp.where(n < 0, -1, entry) == row, 1.0, 0.0)
            place = place + hit
            kinds[face] = kinds[face] + mm_nt(ones, hit.astype(BF))[0:1]
        places.append(place)
    own_place_out[...] = jnp.where(core_number() == 0, places[0], places[1]).astype(BF)
    place = jnp.concatenate(places, axis=1).astype(BF)
    place_out[...] = place
    kinds_out[...] = jnp.concatenate(kinds + [jnp.zeros((2, 256), F32)], axis=0)
    meet_out[...] = mm(place, pick[...]).astype(BF)


def force_kernel(first, second, third, packed, out):
    lamb = first[...] + second[...] + third[...]
    high, low = split(lamb)
    source = one_hot(packed[262:263].astype(jnp.int32) == row_iota((256, 256)))
    out[...] = mm(high, source) + mm(low, source)


def came_columns(first, second):
    return split(jnp.transpose(jnp.concatenate(sides(first, second), axis=0)))


def leave_kernel(
    first, second, base, arrive_pick, send_kinds, trace, force_mine, force_other, select,
    wide_first, wide_second, own_first, own_second,
):
    chosen = [mm(term, arrive_pick[...]).astype(BF) for term in came_columns(first[...], second[...])]
    shown = mm(trace[...], jnp.concatenate(chosen, axis=1))
    sent = base[...] + of_kind(shown[:, :256] + shown[:, 256:], send_kinds[...])
    own = sides(sent[:, :LANES], sent[:, LANES:])
    force = jnp.concatenate(chip_halves(force_mine[...], force_other[...]), axis=1)
    high, low = split(force)
    moved = mm_nt(select[...], high) + mm_nt(select[...], low)
    pieces = sides(moved[0:48], moved[48:96])
    for wide, piece, part in zip((wide_first, wide_second), pieces, own):
        wide[:, 0:192] = piece
        wide[:, 192:256] = jnp.zeros((48, 64), F32)
        wide[:, 256:384] = part
    own_first[...], own_second[...] = own


def near_rates(state, near, interior, trace, lift_two):
    high, low = split(state)
    rates = mm(interior, jnp.concatenate([high, low, high], axis=0))
    shown = mm(trace, jnp.concatenate([high, low], axis=1))
    shown_high, shown_low = split(shown[:, 0:512] + shown[:, 512:1024])
    faces = []
    for device in range(2):
        columns = slice(256 * device, 256 * (device + 1))
        outside_high, outside_low = [], []
        for face in range(6):
            rows = slice(TRACE_ROWS * (face ^ 1), TRACE_ROWS * (face ^ 1) + TRACE_ROWS)
            stacked = jnp.concatenate([shown_high[rows, columns], shown_low[rows, columns]], axis=0)
            found = mm(stacked, near[6 * device + face]).astype(BF)
            outside_high.append(found[:TRACE_ROWS])
            outside_low.append(found[TRACE_ROWS:])
        faces.append(jnp.concatenate(outside_high + outside_low, axis=0))
    return rates + LIFT * mm(lift_two, jnp.concatenate(faces, axis=1))


def weight_of(segment):
    acoustic = lax.axis_index("sec") > 0
    return jnp.where(acoustic, F32(SEGMENT_WEIGHTS[segment]), F32(0.0))


def first_inner_kernel(
    first, second, kept, arrive, force_mine, force_other, keep, near, interior, trace, lift_two,
    pick, send_kinds, state_out, carry_out, force_out, base_out,
):
    high, low = came_columns(first[...], second[...])
    state = kept[...] + (mm(high, arrive[...]) + mm(low, arrive[...]))
    state_out[...] = state
    high, low = split(jnp.concatenate(chip_halves(force_mine[...], force_other[...]), axis=1))
    force = mm_nt(high, keep[...]) + mm_nt(low, keep[...])
    force_out[...] = force
    own = TIME_STEP * near_rates(state, near, interior[...], trace[...], lift_two[...])
    own = jnp.concatenate([own[0:64], own[64:256] + TIME_STEP * force], axis=0)
    carry_out[...] = own
    ahead = state + weight_of(0) * own
    base_out[...] = picked_traces(ahead, pick[...], send_kinds[...], trace[...])


def first_outer_kernel(
    first, second, sent_first, sent_second, kinds, meet, reach, send_kinds, base, trace, arrive_pick,
    stacks_out, first_out, second_out,
):
    stacks = by_kind(
        (first[:, 256:384], second[:, 256:384]), (sent_first[...], sent_second[...]), kinds[...]
    )
    stacks_out[...] = stacks
    shown = LIFT * mm(reach[...], mm(stacks, meet[...]).astype(BF))
    chosen = [
        jnp.concatenate([jnp.zeros((64, 256), BF), mm(term[0:192], arrive_pick[...]).astype(BF)], axis=0)
        for term in came_columns(first[:, 0:256], second[:, 0:256])
    ]
    pushed = mm(trace[...], jnp.concatenate(chosen, axis=1))
    shown = shown + (pushed[:, :256] + pushed[:, 256:])
    sent = base[...] + (weight_of(0) * F32(TIME_STEP)) * of_kind(shown, send_kinds[...])
    first_out[...], second_out[...] = sides(sent[:, :LANES], sent[:, LANES:])


def inner_kernel(segment, state, carry, force, stacks, place, near, interior, trace, lift_two, *refs):
    rates = far_rates(stacks[...], place[...], lift_two[...])
    carry_now = carry[...] + (LIFT * TIME_STEP) * rates
    force = force[...]
    if segment == 1:
        (first, second, arrive), refs = refs[:3], refs[3:]
        high, low = came_columns(first[:, 0:256], second[:, 0:256])
        came = mm(high[0:192], arrive[...]) + mm(low[0:192], arrive[...])
        carry_now = jnp.concatenate([carry_now[0:64], carry_now[64:256] + TIME_STEP * came], axis=0)
        force = force + came
    state_now = state[...] + weight_of(segment - 1) * carry_now
    rates = near_rates(state_now, near, interior[...], trace[...], lift_two[...])
    own = SEGMENT_CARRY[segment] * carry_now + TIME_STEP * rates
    own = jnp.concatenate([own[0:64], own[64:256] + TIME_STEP * force], axis=0)
    ahead = state_now + weight_of(segment) * own
    if segment == 4:
        refs[0][...] = jnp.where(core_number() == 0, ahead[:, 0:256], ahead[:, 256:512])
        return
    (pick, send_kinds, state_out, carry_out, base_out), refs = refs[:5], refs[5:]
    state_out[...] = state_now
    carry_out[...] = own
    base_out[...] = picked_traces(ahead, pick[...], send_kinds[...], trace[...])
    if segment == 1:
        refs[0][...] = force


def outer_kernel(
    segment, first, second, sent_first, sent_second, kinds, meet, reach, send_kinds, base,
    stacks_out, first_out, second_out,
):
    stacks = by_kind((first[...], second[...]), (sent_first[...], sent_second[...]), kinds[...])
    stacks_out[...] = stacks
    shown = mm(reach[...], mm(stacks, meet[...]).astype(BF))
    sent = base[...] + (weight_of(segment) * F32(LIFT * TIME_STEP)) * of_kind(shown, send_kinds[...])
    first_out[...], second_out[...] = sides(sent[:, :LANES], sent[:, LANES:])


def last_kernel(
    first, second, sent_first, sent_second, kinds, own_place, lift_two, ahead, out, held, done
):
    stacks = by_kind((first[...], second[...]), (sent_first[...], sent_second[...]), kinds[...])
    outside = mm(stacks, own_place[...]).astype(BF)
    scale = weight_of(4) * F32(LIFT * TIME_STEP)
    copies = []
    for number, rows in enumerate((slice(0, 128), slice(128, 256))):
        held[rows] = ahead[rows] + scale * mm(lift_two[rows], outside)
        copies.append(pltpu.make_async_copy(held.at[rows], out.at[rows], done.at[number]))
        copies[-1].start()
    for copy in copies:
        copy.wait()


def call(kernel, outs, *args, flops=1 << 20, far=False, scratch=()):
    vmem = pl.BlockSpec(memory_space=pltpu.VMEM)
    size = sum(int(np.prod(a.shape)) * a.dtype.itemsize for a in (*args, *outs))
    return pl.pallas_call(
        kernel,
        out_shape=list(outs),
        in_specs=[vmem] * len(args),
        out_specs=[pl.BlockSpec(memory_space=pl.ANY) if far else vmem] * len(outs),
        scratch_shapes=list(scratch),
        compiler_params=pltpu.CompilerParams(vmem_limit_bytes=32 << 20),
        cost_estimate=pl.CostEstimate(flops=flops, bytes_accessed=size, transcendentals=0),
    )(*args)


def arr(*shape, dtype=F32):
    return jax.ShapeDtypeStruct(shape, dtype)


def trade(first, second, sections):
    count = lax.axis_size("dom")
    came = []
    for value, odd in ((first, 1), (second, 0)):
        pairs = []
        for section in sections:
            for dom in range(count - 2):
                if (dom >> 1) & 1 == odd:
                    low = section * count + dom
                    pairs += [(low, low + 2), (low + 2, low)]
        came.append(lax.ppermute(value, ("sec", "dom"), pairs))
    return came


def swap(value, sections):
    count = lax.axis_size("dom")
    pairs = [(section * count + at, section * count + (at ^ 1)) for section in sections for at in range(count)]
    return lax.ppermute(value, ("sec", "dom"), pairs)


def step(fields, source_map, new_owner, send_list, face_slot):
    cells = fields.reshape(ROWS, ELEMENTS)
    high, low = two_terms(interior_matrix())
    interior = jnp.asarray(np.concatenate([high, high, low], axis=1))
    trace = jnp.asarray(trace_matrix().astype(BF))
    lift_two = jnp.asarray(np.concatenate([lift_matrix()] * 2, axis=1).astype(BF))
    reach = jnp.asarray(np.concatenate([trace_matrix() @ lift_matrix()] * 2, axis=1).astype(BF))
    every = range(lax.axis_size("sec"))
    acoustic = every[1:]
    piece, whole = arr(TRACE_ROWS, LANES), arr(256, 512)

    names = jnp.zeros((264, 256), jnp.int32)
    for part, row, lane in (
        (face_slot, 256, 0),
        (source_map.reshape(1, 256), 262, 0),
        (new_owner.reshape(1, 64), 263, 0),
        (send_list.reshape(1, 96), 263, 128),
    ):
        rows, lanes = part.shape
        edges = ((row, 264 - row - rows, 0), (lane, 256 - lane - lanes, 0))
        names = names + lax.pad(part, jnp.int32(0), edges)
    packed = names.astype(F32) + lax.pad(cells, F32(0.0), ((0, 8, 0), (0, 0, 0)))
    (lamb,) = call(lamb_kernel, [arr(192, 256)], packed)
    lamb_parts = []
    for section in (1, 2, 3):
        lamb_parts.append(lax.ppermute(lamb, "sec", [(0, section)]))
    other = swap(packed, acoustic)
    other_flow = swap(packed, every[:1])
    mates = (packed, other, other_flow)
    *leaving, select, ranks = call(
        depart_kernel,
        [arr(48, 256), arr(48, 256), arr(96, 512, dtype=BF), arr(32, 256)],
        *mates,
    )
    moved = trade(*leaving, every)
    (force_mine,) = call(force_kernel, [arr(192, 256)], *lamb_parts, packed)
    force_other = swap(force_mine, acoustic)
    kept, keep, arrive, pick, send_kinds, arrive_pick, base = call(
        places_kernel,
        [
            whole,
            arr(512, 512, dtype=BF),
            arr(96, 512, dtype=BF),
            arr(512, 256, dtype=BF),
            arr(8, 256),
            arr(96, 256, dtype=BF),
            arr(TRACE_ROWS, 256),
        ],
        *mates,
        ranks,
        trace,
    )
    *wide, own_first, own_second = call(
        leave_kernel,
        [arr(48, 384), arr(48, 384), piece, piece],
        *moved, base, arrive_pick, send_kinds, trace, force_mine, force_other, select,
    )
    sent = [own_first, own_second]
    came = trade(*wide, acoustic)
    near, place, own_place, kinds, meet = call(
        faces_kernel,
        [
            arr(12, 256, 256, dtype=BF),
            arr(256, 512, dtype=BF),
            arr(256, 256, dtype=BF),
            arr(8, 256),
            arr(256, 256, dtype=BF),
        ],
        *mates,
        pick,
    )
    state, carry, force, base = call(
        first_inner_kernel,
        [whole, whole, arr(192, 512), arr(TRACE_ROWS, 256)],
        *moved, kept, arrive, force_mine, force_other, keep, near, interior, trace, lift_two,
        pick, send_kinds,
    )
    sending = [arr(12 * TRACE_ROWS, 256, dtype=BF), piece, piece]
    stacks, *later = call(
        first_outer_kernel,
        sending,
        *came, *sent, kinds, meet, reach, send_kinds, base, trace, arrive_pick,
    )
    extra = [*came, arrive]
    for segment in range(1, 5):
        sent, came = later, trade(*later, acoustic)
        inner = functools.partial(inner_kernel, segment)
        args = [state, carry, force, stacks, place, near, interior, trace, lift_two]
        if segment == 4:
            (ahead,) = call(inner, [arr(256, 256)], *args)
            break
        outs = [whole, whole, arr(TRACE_ROWS, 256)]
        if segment == 1:
            state, carry, base, force = call(
                inner, [*outs, arr(192, 512)], *args, *extra, pick, send_kinds
            )
        else:
            state, carry, base = call(inner, outs, *args, pick, send_kinds)
        stacks, *later = call(
            functools.partial(outer_kernel, segment),
            sending,
            *came, *sent, kinds, meet, reach, send_kinds, base,
        )
    (out,) = call(
        last_kernel,
        [arr(256, 256)],
        *came, *sent, kinds, own_place, lift_two, ahead,
        far=True,
        scratch=(pltpu.VMEM((256, 256), F32), pltpu.SemaphoreType.DMA((2,))),
    )
    return out.reshape(4, 64, ELEMENTS)


def solution(mesh):
    in_specs = (
        P(None, None, ("sec", "dom")),
        P(("sec", "dom")),
        P(("sec", "dom")),
        P(("sec", "dom")),
        P(None, ("sec", "dom")),
    )
    out_specs = P(None, None, ("sec", "dom"))
    return jax.shard_map(step, mesh=mesh, in_specs=in_specs, out_specs=out_specs, check_vma=False)
```

```python
import functools

import jax
import jax.numpy as jnp
import numpy as np
from jax import lax
from jax.experimental import pallas as pl
from jax.experimental.pallas import tpu as pltpu
from jax.sharding import PartitionSpec as P


FACE_CAP = 24
PIECES = 3
LANES = 128
ELEMENTS = 256
ROWS = 256
TRACE_ROWS = 48
LIFT = 3.0
TIME_STEP = 0.12
SEGMENT_CARRY = [
    0.0,
    -567301805773.0 / 1357537059087.0,
    -2404267990393.0 / 2016746695238.0,
    -3550918686646.0 / 2091501179385.0,
    -1275806237668.0 / 842570457699.0,
]
SEGMENT_WEIGHTS = [
    1432997174477.0 / 9575080441755.0,
    5161836677717.0 / 13612068292357.0,
    1720146321549.0 / 2090206949498.0,
    3134564353537.0 / 4481467310338.0,
    2277821191437.0 / 14882151754819.0,
]
BF = jnp.bfloat16
F32 = jnp.float32


def node_derivative():
    points = np.array([-1.0, -1.0 / np.sqrt(5.0), 1.0 / np.sqrt(5.0), 1.0])
    products = np.array(
        [np.prod([points[row] - points[col] for col in range(4) if col != row]) for row in range(4)]
    )
    matrix = np.zeros((4, 4))
    for row in range(4):
        for col in range(4):
            if row != col:
                matrix[row, col] = products[row] / (products[col] * (points[row] - points[col]))
        matrix[row, row] = -np.sum(matrix[row])
    return matrix


def along(matrix, direction):
    eye = np.eye(4)
    parts = [eye, eye, eye]
    parts[direction] = matrix
    return np.kron(np.kron(parts[0], parts[1]), parts[2])


def face_nodes(face):
    direction, side = divmod(face, 2)
    index = np.arange(64).reshape(4, 4, 4)
    return np.take(index, 3 * side, axis=direction).reshape(-1)


def interior_matrix():
    derivative = node_derivative()
    total = np.zeros((256, 256))
    for a in range(3):
        d = along(derivative, a)
        total[0:64, 64 * (a + 1) : 64 * (a + 2)] -= d
        total[64 * (a + 1) : 64 * (a + 2), 0:64] -= d
    for face in range(6):
        a, side = divmod(face, 2)
        sign = 2.0 * side - 1.0
        nodes = face_nodes(face)
        va = 64 * (a + 1) + nodes
        total[nodes, nodes] -= LIFT
        total[nodes, va] += LIFT * sign
        total[va, va] -= LIFT
        total[va, nodes] += LIFT * sign
        for b in range(3):
            if b != a:
                vb = 64 * (b + 1) + nodes
                total[vb, vb] -= LIFT
    return total


def trace_matrix():
    total = np.zeros((6 * TRACE_ROWS, 256))
    for face in range(6):
        a, side = divmod(face, 2)
        sign = 2.0 * side - 1.0
        nodes = face_nodes(face)
        rows = TRACE_ROWS * face + np.arange(16)
        total[rows, nodes] = 1.0
        total[rows, 64 * (a + 1) + nodes] = sign
        for number, b in enumerate([b for b in range(3) if b != a]):
            total[rows + 16 * (number + 1), 64 * (b + 1) + nodes] = 1.0
    return total


def lift_matrix():
    total = np.zeros((256, 6 * TRACE_ROWS))
    for face in range(6):
        a, side = divmod(face, 2)
        sign = 2.0 * side - 1.0
        nodes = face_nodes(face)
        cols = TRACE_ROWS * face + np.arange(16)
        total[nodes, cols] = 1.0
        total[64 * (a + 1) + nodes, cols] = -sign
        for number, b in enumerate([b for b in range(3) if b != a]):
            total[64 * (b + 1) + nodes, cols + 16 * (number + 1)] = 1.0
    return total


def two_terms(matrix):
    high = matrix.astype(np.float32).astype(BF)
    low = (matrix - high.astype(np.float64)).astype(np.float32).astype(BF)
    return high, low


def mm(a, b):
    return lax.dot_general(a, b, (((1,), (0,)), ((), ())), preferred_element_type=F32)


def mm_nt(a, b):
    return lax.dot_general(a, b, (((1,), (1,)), ((), ())), preferred_element_type=F32)


def split(x):
    high = x.astype(BF)
    return high, (x - high.astype(F32)).astype(BF)


def one_hot(mask):
    return jnp.where(mask, 1.0, 0.0).astype(BF)


def rows_named(names, row):
    hit = names.astype(jnp.int32).astype(jnp.int16) == row
    return jnp.where(hit, jnp.ones(row.shape, BF), jnp.zeros(row.shape, BF))


def lane_iota(shape):
    return lax.broadcasted_iota(jnp.int32, shape, 1)


def row_iota(shape):
    return lax.broadcasted_iota(jnp.int32, shape, 0)


def picked_traces(state, pick, kinds, trace):
    high, low = split(state)
    chosen = jnp.concatenate([mm(high, pick).astype(BF), mm(low, pick).astype(BF)], axis=1)
    shown = mm(trace, chosen)
    return of_kind(shown[:, :256] + shown[:, 256:], kinds)


def of_kind(shown, kinds):
    total = jnp.zeros((TRACE_ROWS, 256), F32)
    for face in range(6):
        part = shown[TRACE_ROWS * face : TRACE_ROWS * (face + 1)]
        total = total + jnp.where(kinds[face : face + 1] > 0, part, 0.0)
    return total


def by_kind(came, sent, kinds):
    far = lane_iota((TRACE_ROWS, LANES)) < PIECES * FACE_CAP
    from_left, from_right = sides(*came)
    own_left, own_right = sides(*sent)
    got = jnp.concatenate(
        [jnp.where(far, from_right, own_left), jnp.where(far, from_left, own_right)], axis=1
    )
    chosen = jnp.where(kinds > 0, 1.0, 0.0).astype(BF)
    return jnp.concatenate(
        [term * chosen[face : face + 1] for term in split(got) for face in range(6)], axis=0
    )


def far_rates(stacks, place, lift_two):
    return mm(lift_two, mm(stacks, place).astype(BF))


def sides(first, second):
    odd = ((lax.axis_index("dom") >> 1) & 1) == 1
    return jnp.where(odd, second, first), jnp.where(odd, first, second)


def core_number():
    return lax.axis_index("dom") & 1


def chip_halves(mine, other):
    first = core_number() == 0
    return jnp.where(first, mine, other), jnp.where(first, other, mine)


def difference_along(stride):
    row, col = row_iota((64, 64)), lane_iota((64, 64))
    at, step = (row // stride) & 3, ((col // stride) & 3) - ((row // stride) & 3)
    inner = jnp.where(step == 1, 0.5, jnp.where(step == -1, -0.5, 0.0))
    lower = jnp.where(step == 1, 1.0, jnp.where(step == 0, -1.0, 0.0))
    upper = jnp.where(step == 0, 1.0, jnp.where(step == -1, -1.0, 0.0))
    value = jnp.where(at == 0, lower, jnp.where(at == 3, upper, inner))
    return jnp.where(col - row == step * stride, value, 0.0).astype(BF)


def lamb_kernel(packed, lamb_out):
    slopes = jnp.concatenate([difference_along(stride) for stride in (16, 4, 1)], axis=0)
    v = [packed[64 * a : 64 * (a + 1)] for a in range(3)]
    high, low = split(jnp.concatenate(v, axis=1))
    found = mm(slopes, high) + mm(slopes, low)

    def slope(component, direction):
        return found[64 * direction : 64 * direction + 64, 256 * component : 256 * component + 256]

    w = [
        slope(2, 1) - slope(1, 2),
        slope(0, 2) - slope(2, 0),
        slope(1, 0) - slope(0, 1),
    ]
    rho = packed[192:256]
    lamb_out[0:64] = rho * (w[1] * v[2] - w[2] * v[1])
    lamb_out[64:128] = rho * (w[2] * v[0] - w[0] * v[2])
    lamb_out[128:192] = rho * (w[0] * v[1] - w[1] * v[0])


def group_of(device, offset):
    return 8 * device + {0: 0, -2: 1, -1: 2, 1: 3, 2: 4}[offset]


def start_of(count, device, offset):
    total = jnp.zeros((1, 1), F32)
    for number in (0, -2, -1, 1, 2):
        if number == offset:
            return total
        at = group_of(device, number)
        total = total + count[at : at + 1]


def target_of(members, rank, device, moves):
    total = jnp.full((1, 256), -1.0, F32)
    for offset, base in moves:
        at = group_of(device, offset)
        total = total + members[at : at + 1] * (rank[at : at + 1] + (base + 1.0))
    return total


def depart_kernel(mine, other, other_flow, first_out, second_out, select_out, ranks_out):
    low, high = chip_halves(mine[...], other[...] + other_flow[...])
    first = (lax.axis_index("dom") & -2).astype(F32)
    spread = one_hot((lane_iota((64, 256)) >> 2) == row_iota((64, 256)))
    before = one_hot(row_iota((256, 256)) < lane_iota((256, 256)))
    row8 = row_iota((8, 256))
    wanted = jnp.where(row8 == 0, 0, jnp.where(row8 < 3, row8 - 3, row8 - 2)).astype(F32)
    members = []
    for number, half in enumerate((low, high)):
        owner = half[263:264, 0:64] - (first + number)
        owner = jnp.clip(jnp.broadcast_to(owner, (8, 64)), -8.0, 8.0).astype(BF)
        member = (mm(owner, spread) == wanted) & (row8 < 5)
        members.append(jnp.where(member, 1.0, 0.0))
    members = jnp.concatenate(members, axis=0)
    rank = mm(members.astype(BF), before)
    ranks_out[0:16] = members
    ranks_out[16:32] = rank
    low_target = target_of(members, rank, 0, ((-2, 0.0), (-1, 16.0), (2, 48.0)))
    high_target = target_of(members, rank, 1, ((-2, 32.0), (1, 64.0), (2, 80.0)))
    number = row_iota((96, 256)).astype(F32)
    select = jnp.concatenate([one_hot(low_target == number), one_hot(high_target == number)], axis=1)
    select_out[...] = select
    cells = jnp.concatenate([low[0:256], high[0:256]], axis=1)
    cells_high, cells_low = split(cells)
    sent = mm_nt(select, cells_high) + mm_nt(select, cells_low)
    first_out[...], second_out[...] = sides(sent[0:48], sent[48:96])


def places_kernel(
    mine, other, other_flow, ranks, trace,
    kept_out, keep_out, arrive_out, pick_out, send_kinds_out, arrive_pick_out, base_out,
):
    low, high = chip_halves(mine[...], other[...] + other_flow[...])
    members, rank = ranks[0:16], ranks[16:32]
    count = jnp.sum(members, axis=1, keepdims=True)
    low_place = target_of(members, rank, 0, ((0, 0.0), (1, 256.0 + start_of(count, 1, -1))))
    high_place = target_of(members, rank, 1, ((0, 256.0), (-1, start_of(count, 0, 1))))
    row = row_iota((512, 256)).astype(jnp.int16)
    keep = jnp.concatenate([rows_named(low_place, row), rows_named(high_place, row)], axis=1)
    keep_out[...] = keep
    column = lane_iota((16, 512)).astype(F32)
    number = row_iota((16, 512)).astype(F32)
    blocks = []
    for device, offset in ((0, -2), (0, -1), (1, -2), (0, 2), (1, 1), (1, 2)):
        at = group_of(device, offset)
        begin = start_of(count, device, offset) + 256.0 * device
        blocks.append(one_hot((column - begin == number) & (number < count[at : at + 1])))
    arrive = jnp.concatenate(blocks, axis=0)
    arrive_out[...] = arrive
    cells_high, cells_low = split(jnp.concatenate([low[0:256], high[0:256]], axis=1))
    kept = mm_nt(cells_high, keep) + mm_nt(cells_low, keep)
    kept_out[...] = kept
    lane = lane_iota((8, LANES))
    lists = [jnp.broadcast_to(half[263:264, 128:256], (8, LANES)) for half in (low, high)]
    left = jnp.where(lane < 48, lists[0], pltpu.roll(lists[1], 48, 1))
    right = jnp.where(
        lane < 24,
        pltpu.roll(lists[0], LANES - 72, 1),
        jnp.where(lane < 72, pltpu.roll(lists[1], LANES - 24, 1), pltpu.roll(lists[0], 24, 1)),
    )
    names = jnp.concatenate(
        [jnp.where(lane < 96, left, -1.0), jnp.where(lane < 96, right, -1.0)], axis=1
    ).astype(jnp.int32)
    wide = lane_iota((8, 256))
    second = ((wide >= 48) & (wide < 128)) | ((wide >= 152) & (wide < 200))
    column = jnp.where(names < 0, -1, (names & 255) + jnp.where(second, 256, 0))
    pick = rows_named(column[0:1], row)
    pick_out[...] = pick
    send_kinds = jnp.where((names >> 8) == row_iota((8, 256)), 1.0, 0.0)
    send_kinds_out[...] = send_kinds
    arrive_pick_out[...] = mm(arrive, pick).astype(BF)
    base_out[...] = picked_traces(kept, pick, send_kinds, trace[...])


def faces_kernel(mine, other, other_flow, pick, local_out, place_out, own_place_out, kinds_out, meet_out):
    row = row_iota((256, 256)).astype(jnp.int16)
    ones = jnp.ones((8, 256), BF)
    kinds = [jnp.zeros((1, 256), F32)] * 6
    places = []
    for device, half in enumerate(chip_halves(mine[256:264], other[256:264] + other_flow[256:264])):
        place = jnp.zeros((256, 256), BF)
        for face in range(6):
            where = half[face : face + 1].astype(jnp.int32)
            local_out[6 * device + face] = rows_named(where - ELEMENTS * (face ^ 1), row)
            n = where - 6 * ELEMENTS
            if device == 0:
                entry = jnp.where(n < 48, n + 128, jnp.where(n < 72, n + 24, n - 72))
            else:
                entry = jnp.where(n < 48, n + 176, n - 24)
            hit = rows_named(jnp.where(n < 0, -1, entry), row)
            place = place + hit
            kinds[face] = kinds[face] + mm_nt(ones, hit)[0:1]
        places.append(place)
    own_place_out[...] = jnp.where(core_number() == 0, places[0], places[1])
    place = jnp.concatenate(places, axis=1)
    place_out[...] = place
    kinds_out[...] = jnp.concatenate(kinds + [jnp.zeros((2, 256), F32)], axis=0)
    meet_out[...] = mm(place, pick[...]).astype(BF)


def force_kernel(first, second, third, packed, out):
    lamb = first[...] + second[...] + third[...]
    high, low = split(lamb)
    source = one_hot(packed[262:263].astype(jnp.int32) == row_iota((256, 256)))
    out[...] = mm(high, source) + mm(low, source)


def came_columns(first, second):
    return split(jnp.transpose(jnp.concatenate(sides(first, second), axis=0)))


def leave_kernel(
    first, second, base, arrive_pick, send_kinds, trace, force_mine, force_other, select,
    wide_first, wide_second, own_first, own_second,
):
    chosen = [mm(term, arrive_pick[...]).astype(BF) for term in came_columns(first[...], second[...])]
    shown = mm(trace[...], jnp.concatenate(chosen, axis=1))
    sent = base[...] + of_kind(shown[:, :256] + shown[:, 256:], send_kinds[...])
    own = sides(sent[:, :LANES], sent[:, LANES:])
    force = jnp.concatenate(chip_halves(force_mine[...], force_other[...]), axis=1)
    high, low = split(force)
    moved = mm_nt(select[...], high) + mm_nt(select[...], low)
    pieces = sides(moved[0:48], moved[48:96])
    for wide, piece, part in zip((wide_first, wide_second), pieces, own):
        wide[:, 0:192] = piece
        wide[:, 192:256] = jnp.zeros((48, 64), F32)
        wide[:, 256:384] = part
    own_first[...], own_second[...] = own


def near_rates(state, near, interior, trace, lift_two):
    high, low = split(state)
    rates = mm(interior, jnp.concatenate([high, low, high], axis=0))
    shown = mm(trace, jnp.concatenate([high, low], axis=1))
    shown_high, shown_low = split(shown[:, 0:512] + shown[:, 512:1024])
    faces = []
    for device in range(2):
        columns = slice(256 * device, 256 * (device + 1))
        outside_high, outside_low = [], []
        for face in range(6):
            rows = slice(TRACE_ROWS * (face ^ 1), TRACE_ROWS * (face ^ 1) + TRACE_ROWS)
            stacked = jnp.concatenate([shown_high[rows, columns], shown_low[rows, columns]], axis=0)
            found = mm(stacked, near[6 * device + face]).astype(BF)
            outside_high.append(found[:TRACE_ROWS])
            outside_low.append(found[TRACE_ROWS:])
        faces.append(jnp.concatenate(outside_high + outside_low, axis=0))
    return rates + LIFT * mm(lift_two, jnp.concatenate(faces, axis=1))


def weight_of(segment):
    acoustic = lax.axis_index("sec") > 0
    return jnp.where(acoustic, F32(SEGMENT_WEIGHTS[segment]), F32(0.0))


def first_inner_kernel(
    first, second, kept, arrive, force_mine, force_other, keep, near, interior, trace, lift_two,
    pick, send_kinds, state_out, carry_out, force_out, base_out,
):
    high, low = came_columns(first[...], second[...])
    state = kept[...] + (mm(high, arrive[...]) + mm(low, arrive[...]))
    state_out[...] = state
    high, low = split(jnp.concatenate(chip_halves(force_mine[...], force_other[...]), axis=1))
    force = mm_nt(high, keep[...]) + mm_nt(low, keep[...])
    force_out[...] = force
    own = TIME_STEP * near_rates(state, near, interior[...], trace[...], lift_two[...])
    own = jnp.concatenate([own[0:64], own[64:256] + TIME_STEP * force], axis=0)
    carry_out[...] = own
    ahead = state + weight_of(0) * own
    base_out[...] = picked_traces(ahead, pick[...], send_kinds[...], trace[...])


def first_outer_kernel(
    first, second, sent_first, sent_second, kinds, meet, reach, send_kinds, base, trace, arrive_pick,
    stacks_out, first_out, second_out,
):
    stacks = by_kind(
        (first[:, 256:384], second[:, 256:384]), (sent_first[...], sent_second[...]), kinds[...]
    )
    stacks_out[...] = stacks
    shown = LIFT * mm(reach[...], mm(stacks, meet[...]).astype(BF))
    chosen = [
        jnp.concatenate([jnp.zeros((64, 256), BF), mm(term[0:192], arrive_pick[...]).astype(BF)], axis=0)
        for term in came_columns(first[:, 0:256], second[:, 0:256])
    ]
    pushed = mm(trace[...], jnp.concatenate(chosen, axis=1))
    shown = shown + (pushed[:, :256] + pushed[:, 256:])
    sent = base[...] + (weight_of(0) * F32(TIME_STEP)) * of_kind(shown, send_kinds[...])
    first_out[...], second_out[...] = sides(sent[:, :LANES], sent[:, LANES:])


def inner_kernel(segment, state, carry, force, stacks, place, near, interior, trace, lift_two, *refs):
    rates = far_rates(stacks[...], place[...], lift_two[...])
    carry_now = carry[...] + (LIFT * TIME_STEP) * rates
    force = force[...]
    if segment == 1:
        (first, second, arrive), refs = refs[:3], refs[3:]
        high, low = came_columns(first[:, 0:256], second[:, 0:256])
        came = mm(high[0:192], arrive[...]) + mm(low[0:192], arrive[...])
        carry_now = jnp.concatenate([carry_now[0:64], carry_now[64:256] + TIME_STEP * came], axis=0)
        force = force + came
    state_now = state[...] + weight_of(segment - 1) * carry_now
    rates = near_rates(state_now, near, interior[...], trace[...], lift_two[...])
    own = SEGMENT_CARRY[segment] * carry_now + TIME_STEP * rates
    own = jnp.concatenate([own[0:64], own[64:256] + TIME_STEP * force], axis=0)
    ahead = state_now + weight_of(segment) * own
    if segment == 4:
        refs[0][...] = jnp.where(core_number() == 0, ahead[:, 0:256], ahead[:, 256:512])
        return
    (pick, send_kinds, state_out, carry_out, base_out), refs = refs[:5], refs[5:]
    state_out[...] = state_now
    carry_out[...] = own
    base_out[...] = picked_traces(ahead, pick[...], send_kinds[...], trace[...])
    if segment == 1:
        refs[0][...] = force


def outer_kernel(
    segment, first, second, sent_first, sent_second, kinds, meet, reach, send_kinds, base,
    stacks_out, first_out, second_out,
):
    stacks = by_kind((first[...], second[...]), (sent_first[...], sent_second[...]), kinds[...])
    stacks_out[...] = stacks
    shown = mm(reach[...], mm(stacks, meet[...]).astype(BF))
    sent = base[...] + (weight_of(segment) * F32(LIFT * TIME_STEP)) * of_kind(shown, send_kinds[...])
    first_out[...], second_out[...] = sides(sent[:, :LANES], sent[:, LANES:])


def last_kernel(
    first, second, sent_first, sent_second, kinds, own_place, lift_two, ahead, out, held, done
):
    stacks = by_kind((first[...], second[...]), (sent_first[...], sent_second[...]), kinds[...])
    outside = mm(stacks, own_place[...]).astype(BF)
    scale = weight_of(4) * F32(LIFT * TIME_STEP)
    copies = []
    for number, rows in enumerate((slice(0, 128), slice(128, 256))):
        held[rows] = ahead[rows] + scale * mm(lift_two[rows], outside)
        copies.append(pltpu.make_async_copy(held.at[rows], out.at[rows], done.at[number]))
        copies[-1].start()
    for copy in copies:
        copy.wait()


def call(kernel, outs, *args, flops=1 << 20, far=False, scratch=()):
    vmem = pl.BlockSpec(memory_space=pltpu.VMEM)
    size = sum(int(np.prod(a.shape)) * a.dtype.itemsize for a in (*args, *outs))
    return pl.pallas_call(
        kernel,
        out_shape=list(outs),
        in_specs=[vmem] * len(args),
        out_specs=[pl.BlockSpec(memory_space=pl.ANY) if far else vmem] * len(outs),
        scratch_shapes=list(scratch),
        compiler_params=pltpu.CompilerParams(vmem_limit_bytes=32 << 20),
        cost_estimate=pl.CostEstimate(flops=flops, bytes_accessed=size, transcendentals=0),
    )(*args)


def arr(*shape, dtype=F32):
    return jax.ShapeDtypeStruct(shape, dtype)


def trade(first, second, sections):
    count = lax.axis_size("dom")
    came = []
    for value, odd in ((first, 1), (second, 0)):
        pairs = []
        for section in sections:
            for dom in range(count - 2):
                if (dom >> 1) & 1 == odd:
                    low = section * count + dom
                    pairs += [(low, low + 2), (low + 2, low)]
        came.append(lax.ppermute(value, ("sec", "dom"), pairs))
    return came


def swap(value, sections):
    count = lax.axis_size("dom")
    pairs = [(section * count + at, section * count + (at ^ 1)) for section in sections for at in range(count)]
    return lax.ppermute(value, ("sec", "dom"), pairs)


def step(fields, source_map, new_owner, send_list, face_slot):
    cells = fields.reshape(ROWS, ELEMENTS)
    high, low = two_terms(interior_matrix())
    interior = jnp.asarray(np.concatenate([high, high, low], axis=1))
    trace = jnp.asarray(trace_matrix().astype(BF))
    lift_two = jnp.asarray(np.concatenate([lift_matrix()] * 2, axis=1).astype(BF))
    reach = jnp.asarray(np.concatenate([trace_matrix() @ lift_matrix()] * 2, axis=1).astype(BF))
    every = range(lax.axis_size("sec"))
    acoustic = every[1:]
    piece, whole = arr(TRACE_ROWS, LANES), arr(256, 512)

    names = jnp.zeros((264, 256), jnp.int32)
    for part, row, lane in (
        (face_slot, 256, 0),
        (source_map.reshape(1, 256), 262, 0),
        (new_owner.reshape(1, 64), 263, 0),
        (send_list.reshape(1, 96), 263, 128),
    ):
        rows, lanes = part.shape
        edges = ((row, 264 - row - rows, 0), (lane, 256 - lane - lanes, 0))
        names = names + lax.pad(part, jnp.int32(0), edges)
    packed = names.astype(F32) + lax.pad(cells, F32(0.0), ((0, 8, 0), (0, 0, 0)))
    (lamb,) = call(lamb_kernel, [arr(192, 256)], packed)
    lamb_parts = []
    for section in (1, 2, 3):
        lamb_parts.append(lax.ppermute(lamb, "sec", [(0, section)]))
    other = swap(packed, acoustic)
    other_flow = swap(packed, every[:1])
    mates = (packed, other, other_flow)
    *leaving, select, ranks = call(
        depart_kernel,
        [arr(48, 256), arr(48, 256), arr(96, 512, dtype=BF), arr(32, 256)],
        *mates,
    )
    moved = trade(*leaving, every)
    (force_mine,) = call(force_kernel, [arr(192, 256)], *lamb_parts, packed)
    force_other = swap(force_mine, acoustic)
    kept, keep, arrive, pick, send_kinds, arrive_pick, base = call(
        places_kernel,
        [
            whole,
            arr(512, 512, dtype=BF),
            arr(96, 512, dtype=BF),
            arr(512, 256, dtype=BF),
            arr(8, 256),
            arr(96, 256, dtype=BF),
            arr(TRACE_ROWS, 256),
        ],
        *mates,
        ranks,
        trace,
    )
    *wide, own_first, own_second = call(
        leave_kernel,
        [arr(48, 384), arr(48, 384), piece, piece],
        *moved, base, arrive_pick, send_kinds, trace, force_mine, force_other, select,
    )
    sent = [own_first, own_second]
    came = trade(*wide, acoustic)
    near, place, own_place, kinds, meet = call(
        faces_kernel,
        [
            arr(12, 256, 256, dtype=BF),
            arr(256, 512, dtype=BF),
            arr(256, 256, dtype=BF),
            arr(8, 256),
            arr(256, 256, dtype=BF),
        ],
        *mates,
        pick,
    )
    state, carry, force, base = call(
        first_inner_kernel,
        [whole, whole, arr(192, 512), arr(TRACE_ROWS, 256)],
        *moved, kept, arrive, force_mine, force_other, keep, near, interior, trace, lift_two,
        pick, send_kinds,
    )
    sending = [arr(12 * TRACE_ROWS, 256, dtype=BF), piece, piece]
    stacks, *later = call(
        first_outer_kernel,
        sending,
        *came, *sent, kinds, meet, reach, send_kinds, base, trace, arrive_pick,
    )
    extra = [*came, arrive]
    for segment in range(1, 5):
        sent, came = later, trade(*later, acoustic)
        inner = functools.partial(inner_kernel, segment)
        args = [state, carry, force, stacks, place, near, interior, trace, lift_two]
        if segment == 4:
            (ahead,) = call(inner, [arr(256, 256)], *args)
            break
        outs = [whole, whole, arr(TRACE_ROWS, 256)]
        if segment == 1:
            state, carry, base, force = call(
                inner, [*outs, arr(192, 512)], *args, *extra, pick, send_kinds
            )
        else:
            state, carry, base = call(inner, outs, *args, pick, send_kinds)
        stacks, *later = call(
            functools.partial(outer_kernel, segment),
            sending,
            *came, *sent, kinds, meet, reach, send_kinds, base,
        )
    (out,) = call(
        last_kernel,
        [arr(256, 256)],
        *came, *sent, kinds, own_place, lift_two, ahead,
        far=True,
        scratch=(pltpu.VMEM((256, 256), F32), pltpu.SemaphoreType.DMA((2,))),
    )
    return out.reshape(4, 64, ELEMENTS)


def solution(mesh):
    in_specs = (
        P(None, None, ("sec", "dom")),
        P(("sec", "dom")),
        P(("sec", "dom")),
        P(("sec", "dom")),
        P(None, ("sec", "dom")),
    )
    out_specs = P(None, None, ("sec", "dom"))
    return jax.shard_map(step, mesh=mesh, in_specs=in_specs, out_specs=out_specs, check_vma=False)
```

```python
import functools

import jax
import jax.numpy as jnp
import numpy as np
from jax import lax
from jax.experimental import pallas as pl
from jax.experimental.pallas import tpu as pltpu
from jax.sharding import PartitionSpec as P


FACE_CAP = 24
PIECES = 3
LANES = 128
ELEMENTS = 256
ROWS = 256
TRACE_ROWS = 48
LIFT = 3.0
TIME_STEP = 0.12
SEGMENT_CARRY = [
    0.0,
    -567301805773.0 / 1357537059087.0,
    -2404267990393.0 / 2016746695238.0,
    -3550918686646.0 / 2091501179385.0,
    -1275806237668.0 / 842570457699.0,
]
SEGMENT_WEIGHTS = [
    1432997174477.0 / 9575080441755.0,
    5161836677717.0 / 13612068292357.0,
    1720146321549.0 / 2090206949498.0,
    3134564353537.0 / 4481467310338.0,
    2277821191437.0 / 14882151754819.0,
]
BF = jnp.bfloat16
F32 = jnp.float32


def node_derivative():
    points = np.array([-1.0, -1.0 / np.sqrt(5.0), 1.0 / np.sqrt(5.0), 1.0])
    products = np.array(
        [np.prod([points[row] - points[col] for col in range(4) if col != row]) for row in range(4)]
    )
    matrix = np.zeros((4, 4))
    for row in range(4):
        for col in range(4):
            if row != col:
                matrix[row, col] = products[row] / (products[col] * (points[row] - points[col]))
        matrix[row, row] = -np.sum(matrix[row])
    return matrix


def along(matrix, direction):
    eye = np.eye(4)
    parts = [eye, eye, eye]
    parts[direction] = matrix
    return np.kron(np.kron(parts[0], parts[1]), parts[2])


def face_nodes(face):
    direction, side = divmod(face, 2)
    index = np.arange(64).reshape(4, 4, 4)
    return np.take(index, 3 * side, axis=direction).reshape(-1)


def interior_matrix():
    derivative = node_derivative()
    total = np.zeros((256, 256))
    for a in range(3):
        d = along(derivative, a)
        total[0:64, 64 * (a + 1) : 64 * (a + 2)] -= d
        total[64 * (a + 1) : 64 * (a + 2), 0:64] -= d
    for face in range(6):
        a, side = divmod(face, 2)
        sign = 2.0 * side - 1.0
        nodes = face_nodes(face)
        va = 64 * (a + 1) + nodes
        total[nodes, nodes] -= LIFT
        total[nodes, va] += LIFT * sign
        total[va, va] -= LIFT
        total[va, nodes] += LIFT * sign
        for b in range(3):
            if b != a:
                vb = 64 * (b + 1) + nodes
                total[vb, vb] -= LIFT
    return total


def trace_matrix():
    total = np.zeros((6 * TRACE_ROWS, 256))
    for face in range(6):
        a, side = divmod(face, 2)
        sign = 2.0 * side - 1.0
        nodes = face_nodes(face)
        rows = TRACE_ROWS * face + np.arange(16)
        total[rows, nodes] = 1.0
        total[rows, 64 * (a + 1) + nodes] = sign
        for number, b in enumerate([b for b in range(3) if b != a]):
            total[rows + 16 * (number + 1), 64 * (b + 1) + nodes] = 1.0
    return total


def lift_matrix():
    total = np.zeros((256, 6 * TRACE_ROWS))
    for face in range(6):
        a, side = divmod(face, 2)
        sign = 2.0 * side - 1.0
        nodes = face_nodes(face)
        cols = TRACE_ROWS * face + np.arange(16)
        total[nodes, cols] = 1.0
        total[64 * (a + 1) + nodes, cols] = -sign
        for number, b in enumerate([b for b in range(3) if b != a]):
            total[64 * (b + 1) + nodes, cols + 16 * (number + 1)] = 1.0
    return total


def two_terms(matrix):
    high = matrix.astype(np.float32).astype(BF)
    low = (matrix - high.astype(np.float64)).astype(np.float32).astype(BF)
    return high, low


def mm(a, b):
    return lax.dot_general(a, b, (((1,), (0,)), ((), ())), preferred_element_type=F32)


def mm_nt(a, b):
    return lax.dot_general(a, b, (((1,), (1,)), ((), ())), preferred_element_type=F32)


def split(x):
    high = x.astype(BF)
    return high, (x - high.astype(F32)).astype(BF)


def one_hot(mask):
    return jnp.where(mask, 1.0, 0.0).astype(BF)


def rows_named(names, row):
    hit = names.astype(jnp.int32).astype(jnp.int16) == row
    return jnp.where(hit, jnp.ones(row.shape, BF), jnp.zeros(row.shape, BF))


def lane_iota(shape):
    return lax.broadcasted_iota(jnp.int32, shape, 1)


def row_iota(shape):
    return lax.broadcasted_iota(jnp.int32, shape, 0)


def picked_traces(state, pick, kinds, trace):
    high, low = split(state)
    chosen = jnp.concatenate([mm(high, pick).astype(BF), mm(low, pick).astype(BF)], axis=1)
    shown = mm(trace, chosen)
    return of_kind(shown[:, :256] + shown[:, 256:], kinds)


def of_kind(shown, kinds):
    total = jnp.zeros((TRACE_ROWS, 256), F32)
    for face in range(6):
        part = shown[TRACE_ROWS * face : TRACE_ROWS * (face + 1)]
        total = total + jnp.where(kinds[face : face + 1] > 0, part, 0.0)
    return total


def by_kind(came, sent, kinds):
    far = lane_iota((TRACE_ROWS, LANES)) < PIECES * FACE_CAP
    from_left, from_right = sides(*came)
    own_left, own_right = sides(*sent)
    got = jnp.concatenate(
        [jnp.where(far, from_right, own_left), jnp.where(far, from_left, own_right)], axis=1
    )
    chosen = jnp.where(kinds > 0, 1.0, 0.0).astype(BF)
    return jnp.concatenate(
        [term * chosen[face : face + 1] for term in split(got) for face in range(6)], axis=0
    )


def far_rates(stacks, place, lift_two):
    return mm(lift_two, mm(stacks, place).astype(BF))


def sides(first, second):
    odd = ((lax.axis_index("dom") >> 1) & 1) == 1
    return jnp.where(odd, second, first), jnp.where(odd, first, second)


def core_number():
    return lax.axis_index("dom") & 1


def chip_halves(mine, other):
    first = core_number() == 0
    return jnp.where(first, mine, other), jnp.where(first, other, mine)


def difference_along(stride):
    row, col = row_iota((64, 64)), lane_iota((64, 64))
    at, step = (row // stride) & 3, ((col // stride) & 3) - ((row // stride) & 3)
    inner = jnp.where(step == 1, 0.5, jnp.where(step == -1, -0.5, 0.0))
    lower = jnp.where(step == 1, 1.0, jnp.where(step == 0, -1.0, 0.0))
    upper = jnp.where(step == 0, 1.0, jnp.where(step == -1, -1.0, 0.0))
    value = jnp.where(at == 0, lower, jnp.where(at == 3, upper, inner))
    return jnp.where(col - row == step * stride, value, 0.0).astype(BF)


def lamb_kernel(packed, lamb_out):
    slopes = jnp.concatenate([difference_along(stride) for stride in (16, 4, 1)], axis=0)
    v = [packed[64 * a : 64 * (a + 1)] for a in range(3)]
    high, low = split(jnp.concatenate(v, axis=1))
    found = mm(slopes, high) + mm(slopes, low)

    def slope(component, direction):
        return found[64 * direction : 64 * direction + 64, 256 * component : 256 * component + 256]

    w = [
        slope(2, 1) - slope(1, 2),
        slope(0, 2) - slope(2, 0),
        slope(1, 0) - slope(0, 1),
    ]
    rho = packed[192:256]
    lamb_out[0:64] = rho * (w[1] * v[2] - w[2] * v[1])
    lamb_out[64:128] = rho * (w[2] * v[0] - w[0] * v[2])
    lamb_out[128:192] = rho * (w[0] * v[1] - w[1] * v[0])


def group_of(device, offset):
    return 8 * device + {0: 0, -2: 1, -1: 2, 1: 3, 2: 4}[offset]


def start_of(count, device, offset):
    total = jnp.zeros((1, 1), F32)
    for number in (0, -2, -1, 1, 2):
        if number == offset:
            return total
        at = group_of(device, number)
        total = total + count[at : at + 1]


def target_of(members, rank, device, moves):
    total = jnp.full((1, 256), -1.0, F32)
    for offset, base in moves:
        at = group_of(device, offset)
        total = total + members[at : at + 1] * (rank[at : at + 1] + (base + 1.0))
    return total


def depart_kernel(mine, other, other_flow, first_out, second_out, select_out, ranks_out):
    low, high = chip_halves(mine[...], other[...] + other_flow[...])
    first = (lax.axis_index("dom") & -2).astype(F32)
    spread = one_hot((lane_iota((64, 256)) >> 2) == row_iota((64, 256)))
    before = one_hot(row_iota((256, 256)) < lane_iota((256, 256)))
    row8 = row_iota((8, 256))
    wanted = jnp.where(row8 == 0, 0, jnp.where(row8 < 3, row8 - 3, row8 - 2)).astype(F32)
    members = []
    for number, half in enumerate((low, high)):
        owner = half[263:264, 0:64] - (first + number)
        owner = jnp.clip(jnp.broadcast_to(owner, (8, 64)), -8.0, 8.0).astype(BF)
        member = (mm(owner, spread) == wanted) & (row8 < 5)
        members.append(jnp.where(member, 1.0, 0.0))
    members = jnp.concatenate(members, axis=0)
    rank = mm(members.astype(BF), before)
    ranks_out[0:16] = members
    ranks_out[16:32] = rank
    low_target = target_of(members, rank, 0, ((-2, 0.0), (-1, 16.0), (2, 48.0)))
    high_target = target_of(members, rank, 1, ((-2, 32.0), (1, 64.0), (2, 80.0)))
    number = row_iota((96, 256)).astype(F32)
    select = jnp.concatenate([one_hot(low_target == number), one_hot(high_target == number)], axis=1)
    select_out[...] = select
    cells = jnp.concatenate([low[0:256], high[0:256]], axis=1)
    cells_high, cells_low = split(cells)
    sent = mm_nt(select, cells_high) + mm_nt(select, cells_low)
    first_out[...], second_out[...] = sides(sent[0:48], sent[48:96])


def places_kernel(
    mine, other, other_flow, ranks, trace,
    kept_out, keep_out, arrive_out, pick_out, send_kinds_out, arrive_pick_out, base_out,
):
    low, high = chip_halves(mine[...], other[...] + other_flow[...])
    members, rank = ranks[0:16], ranks[16:32]
    count = jnp.sum(members, axis=1, keepdims=True)
    low_place = target_of(members, rank, 0, ((0, 0.0), (1, 256.0 + start_of(count, 1, -1))))
    high_place = target_of(members, rank, 1, ((0, 256.0), (-1, start_of(count, 0, 1))))
    row = row_iota((512, 256)).astype(jnp.int16)
    keep = jnp.concatenate([rows_named(low_place, row), rows_named(high_place, row)], axis=1)
    keep_out[...] = keep
    column = lane_iota((16, 512)).astype(F32)
    number = row_iota((16, 512)).astype(F32)
    blocks = []
    for device, offset in ((0, -2), (0, -1), (1, -2), (0, 2), (1, 1), (1, 2)):
        at = group_of(device, offset)
        begin = start_of(count, device, offset) + 256.0 * device
        blocks.append(one_hot((column - begin == number) & (number < count[at : at + 1])))
    arrive = jnp.concatenate(blocks, axis=0)
    arrive_out[...] = arrive
    cells_high, cells_low = split(jnp.concatenate([low[0:256], high[0:256]], axis=1))
    kept = mm_nt(cells_high, keep) + mm_nt(cells_low, keep)
    kept_out[...] = kept
    lane = lane_iota((8, LANES))
    lists = [jnp.broadcast_to(half[263:264, 128:256], (8, LANES)) for half in (low, high)]
    left = jnp.where(lane < 48, lists[0], pltpu.roll(lists[1], 48, 1))
    right = jnp.where(
        lane < 24,
        pltpu.roll(lists[0], LANES - 72, 1),
        jnp.where(lane < 72, pltpu.roll(lists[1], LANES - 24, 1), pltpu.roll(lists[0], 24, 1)),
    )
    names = jnp.concatenate(
        [jnp.where(lane < 96, left, -1.0), jnp.where(lane < 96, right, -1.0)], axis=1
    ).astype(jnp.int32)
    wide = lane_iota((8, 256))
    second = ((wide >= 48) & (wide < 128)) | ((wide >= 152) & (wide < 200))
    column = jnp.where(names < 0, -1, (names & 255) + jnp.where(second, 256, 0))
    pick = rows_named(column[0:1], row)
    pick_out[...] = pick
    send_kinds = jnp.where((names >> 8) == row_iota((8, 256)), 1.0, 0.0)
    send_kinds_out[...] = send_kinds
    arrive_pick_out[...] = mm(arrive, pick).astype(BF)
    base_out[...] = picked_traces(kept, pick, send_kinds, trace[...])


def faces_kernel(mine, other, other_flow, pick, local_out, place_out, own_place_out, kinds_out, meet_out):
    row = row_iota((256, 256)).astype(jnp.int16)
    ones = jnp.ones((8, 256), BF)
    kinds = [jnp.zeros((1, 256), F32)] * 6
    places = []
    for device, half in enumerate(chip_halves(mine[256:264], other[256:264] + other_flow[256:264])):
        place = jnp.zeros((256, 256), BF)
        for face in range(6):
            where = half[face : face + 1].astype(jnp.int32)
            local_out[6 * device + face] = rows_named(where - ELEMENTS * (face ^ 1), row)
            n = where - 6 * ELEMENTS
            if device == 0:
                entry = jnp.where(n < 48, n + 128, jnp.where(n < 72, n + 24, n - 72))
            else:
                entry = jnp.where(n < 48, n + 176, n - 24)
            hit = rows_named(jnp.where(n < 0, -1, entry), row)
            place = place + hit
            kinds[face] = kinds[face] + mm_nt(ones, hit)[0:1]
        places.append(place)
    own_place_out[...] = jnp.where(core_number() == 0, places[0], places[1])
    place = jnp.concatenate(places, axis=1)
    place_out[...] = place
    kinds_out[...] = jnp.concatenate(kinds + [jnp.zeros((2, 256), F32)], axis=0)
    meet_out[...] = mm(place, pick[...]).astype(BF)


def force_kernel(first, second, third, packed, out):
    lamb = first[...] + second[...] + third[...]
    high, low = split(lamb)
    source = one_hot(packed[262:263].astype(jnp.int32) == row_iota((256, 256)))
    out[...] = mm(high, source) + mm(low, source)


def came_columns(first, second):
    return split(jnp.transpose(jnp.concatenate(sides(first, second), axis=0)))


def leave_kernel(
    first, second, base, arrive_pick, send_kinds, trace, force_mine, force_other, select,
    wide_first, wide_second, own_first, own_second,
):
    chosen = [mm(term, arrive_pick[...]).astype(BF) for term in came_columns(first[...], second[...])]
    shown = mm(trace[...], jnp.concatenate(chosen, axis=1))
    sent = base[...] + of_kind(shown[:, :256] + shown[:, 256:], send_kinds[...])
    own = sides(sent[:, :LANES], sent[:, LANES:])
    force = jnp.concatenate(chip_halves(force_mine[...], force_other[...]), axis=1)
    high, low = split(force)
    moved = mm_nt(select[...], high) + mm_nt(select[...], low)
    pieces = sides(moved[0:48], moved[48:96])
    for wide, piece, part in zip((wide_first, wide_second), pieces, own):
        wide[:, 0:192] = piece
        wide[:, 192:256] = jnp.zeros((48, 64), F32)
        wide[:, 256:384] = part
    own_first[...], own_second[...] = own


def near_rates(state, near, interior, trace, lift_two):
    high, low = split(state)
    rates = mm(interior, jnp.concatenate([high, low, high], axis=0))
    shown = mm(trace, jnp.concatenate([high, low], axis=1))
    shown_high, shown_low = split(shown[:, 0:512] + shown[:, 512:1024])
    faces = []
    for device in range(2):
        columns = slice(256 * device, 256 * (device + 1))
        outside_high, outside_low = [], []
        for face in range(6):
            rows = slice(TRACE_ROWS * (face ^ 1), TRACE_ROWS * (face ^ 1) + TRACE_ROWS)
            stacked = jnp.concatenate([shown_high[rows, columns], shown_low[rows, columns]], axis=0)
            found = mm(stacked, near[6 * device + face]).astype(BF)
            outside_high.append(found[:TRACE_ROWS])
            outside_low.append(found[TRACE_ROWS:])
        faces.append(jnp.concatenate(outside_high + outside_low, axis=0))
    return rates + LIFT * mm(lift_two, jnp.concatenate(faces, axis=1))


def weight_of(segment):
    acoustic = lax.axis_index("sec") > 0
    return jnp.where(acoustic, F32(SEGMENT_WEIGHTS[segment]), F32(0.0))


def first_inner_kernel(
    first, second, kept, arrive, force_mine, force_other, keep, near, interior, trace, lift_two,
    pick, send_kinds, state_out, carry_out, force_out, base_out,
):
    high, low = came_columns(first[...], second[...])
    state = kept[...] + (mm(high, arrive[...]) + mm(low, arrive[...]))
    state_out[...] = state
    high, low = split(jnp.concatenate(chip_halves(force_mine[...], force_other[...]), axis=1))
    force = mm_nt(high, keep[...]) + mm_nt(low, keep[...])
    force_out[...] = force
    own = TIME_STEP * near_rates(state, near, interior[...], trace[...], lift_two[...])
    own = jnp.concatenate([own[0:64], own[64:256] + TIME_STEP * force], axis=0)
    carry_out[...] = own
    ahead = state + weight_of(0) * own
    base_out[...] = picked_traces(ahead, pick[...], send_kinds[...], trace[...])


def first_outer_kernel(
    first, second, sent_first, sent_second, kinds, meet, reach_force, send_kinds, base, arrive_pick,
    stacks_out, first_out, second_out,
):
    stacks = by_kind(
        (first[:, 256:384], second[:, 256:384]), (sent_first[...], sent_second[...]), kinds[...]
    )
    stacks_out[...] = stacks
    parts = [mm(stacks, meet[...]).astype(BF)]
    for term in came_columns(first[:, 0:256], second[:, 0:256]):
        parts.append(mm(term[0:192], arrive_pick[...]).astype(BF))
    shown = mm(reach_force[...], jnp.concatenate(parts, axis=0))
    sent = base[...] + (weight_of(0) * F32(TIME_STEP)) * of_kind(shown, send_kinds[...])
    first_out[...], second_out[...] = sides(sent[:, :LANES], sent[:, LANES:])


def inner_kernel(segment, state, carry, force, stacks, place, near, interior, trace, lift_two, *refs):
    rates = far_rates(stacks[...], place[...], lift_two[...])
    carry_now = carry[...] + (LIFT * TIME_STEP) * rates
    force = force[...]
    if segment == 1:
        (first, second, arrive), refs = refs[:3], refs[3:]
        high, low = came_columns(first[:, 0:256], second[:, 0:256])
        came = mm(high[0:192], arrive[...]) + mm(low[0:192], arrive[...])
        carry_now = jnp.concatenate([carry_now[0:64], carry_now[64:256] + TIME_STEP * came], axis=0)
        force = force + came
    state_now = state[...] + weight_of(segment - 1) * carry_now
    rates = near_rates(state_now, near, interior[...], trace[...], lift_two[...])
    own = SEGMENT_CARRY[segment] * carry_now + TIME_STEP * rates
    own = jnp.concatenate([own[0:64], own[64:256] + TIME_STEP * force], axis=0)
    ahead = state_now + weight_of(segment) * own
    if segment == 4:
        refs[0][...] = jnp.where(core_number() == 0, ahead[:, 0:256], ahead[:, 256:512])
        return
    (pick, send_kinds, state_out, carry_out, base_out), refs = refs[:5], refs[5:]
    state_out[...] = state_now
    carry_out[...] = own
    base_out[...] = picked_traces(ahead, pick[...], send_kinds[...], trace[...])
    if segment == 1:
        refs[0][...] = force


def outer_kernel(
    segment, first, second, sent_first, sent_second, kinds, meet, reach, send_kinds, base,
    stacks_out, first_out, second_out,
):
    stacks = by_kind((first[...], second[...]), (sent_first[...], sent_second[...]), kinds[...])
    stacks_out[...] = stacks
    shown = mm(reach[...], mm(stacks, meet[...]).astype(BF))
    sent = base[...] + (weight_of(segment) * F32(LIFT * TIME_STEP)) * of_kind(shown, send_kinds[...])
    first_out[...], second_out[...] = sides(sent[:, :LANES], sent[:, LANES:])


def last_kernel(
    first, second, sent_first, sent_second, kinds, own_place, lift_two, ahead, out, held, done
):
    stacks = by_kind((first[...], second[...]), (sent_first[...], sent_second[...]), kinds[...])
    outside = mm(stacks, own_place[...]).astype(BF)
    scale = weight_of(4) * F32(LIFT * TIME_STEP)
    copies = []
    for number, rows in enumerate((slice(0, 128), slice(128, 256))):
        held[rows] = ahead[rows] + scale * mm(lift_two[rows], outside)
        copies.append(pltpu.make_async_copy(held.at[rows], out.at[rows], done.at[number]))
        copies[-1].start()
    for copy in copies:
        copy.wait()


def call(kernel, outs, *args, flops=1 << 20, far=False, scratch=()):
    vmem = pl.BlockSpec(memory_space=pltpu.VMEM)
    size = sum(int(np.prod(a.shape)) * a.dtype.itemsize for a in (*args, *outs))
    return pl.pallas_call(
        kernel,
        out_shape=list(outs),
        in_specs=[vmem] * len(args),
        out_specs=[pl.BlockSpec(memory_space=pl.ANY) if far else vmem] * len(outs),
        scratch_shapes=list(scratch),
        compiler_params=pltpu.CompilerParams(vmem_limit_bytes=32 << 20),
        cost_estimate=pl.CostEstimate(flops=flops, bytes_accessed=size, transcendentals=0),
    )(*args)


def arr(*shape, dtype=F32):
    return jax.ShapeDtypeStruct(shape, dtype)


def trade(first, second, sections):
    count = lax.axis_size("dom")
    came = []
    for value, odd in ((first, 1), (second, 0)):
        pairs = []
        for section in sections:
            for dom in range(count - 2):
                if (dom >> 1) & 1 == odd:
                    low = section * count + dom
                    pairs += [(low, low + 2), (low + 2, low)]
        came.append(lax.ppermute(value, ("sec", "dom"), pairs))
    return came


def swap(value, sections):
    count = lax.axis_size("dom")
    pairs = [(section * count + at, section * count + (at ^ 1)) for section in sections for at in range(count)]
    return lax.ppermute(value, ("sec", "dom"), pairs)


def step(fields, source_map, new_owner, send_list, face_slot):
    cells = fields.reshape(ROWS, ELEMENTS)
    high, low = two_terms(interior_matrix())
    interior = jnp.asarray(np.concatenate([high, high, low], axis=1))
    trace = jnp.asarray(trace_matrix().astype(BF))
    lift_two = jnp.asarray(np.concatenate([lift_matrix()] * 2, axis=1).astype(BF))
    across = np.concatenate([trace_matrix() @ lift_matrix()] * 2, axis=1)
    reach = jnp.asarray(across.astype(BF))
    pushed = [trace_matrix()[:, 64:256]] * 2
    reach_force = jnp.asarray(np.concatenate([LIFT * across, *pushed], axis=1).astype(BF))
    every = range(lax.axis_size("sec"))
    acoustic = every[1:]
    piece, whole = arr(TRACE_ROWS, LANES), arr(256, 512)

    names = jnp.zeros((264, 256), jnp.int32)
    for part, row, lane in (
        (face_slot, 256, 0),
        (source_map.reshape(1, 256), 262, 0),
        (new_owner.reshape(1, 64), 263, 0),
        (send_list.reshape(1, 96), 263, 128),
    ):
        rows, lanes = part.shape
        edges = ((row, 264 - row - rows, 0), (lane, 256 - lane - lanes, 0))
        names = names + lax.pad(part, jnp.int32(0), edges)
    packed = names.astype(F32) + lax.pad(cells, F32(0.0), ((0, 8, 0), (0, 0, 0)))
    (lamb,) = call(lamb_kernel, [arr(192, 256)], packed)
    lamb_parts = []
    for section in (1, 2, 3):
        lamb_parts.append(lax.ppermute(lamb, "sec", [(0, section)]))
    other = swap(packed, acoustic)
    other_flow = swap(packed, every[:1])
    mates = (packed, other, other_flow)
    *leaving, select, ranks = call(
        depart_kernel,
        [arr(48, 256), arr(48, 256), arr(96, 512, dtype=BF), arr(32, 256)],
        *mates,
    )
    moved = trade(*leaving, every)
    (force_mine,) = call(force_kernel, [arr(192, 256)], *lamb_parts, packed)
    force_other = swap(force_mine, acoustic)
    kept, keep, arrive, pick, send_kinds, arrive_pick, base = call(
        places_kernel,
        [
            whole,
            arr(512, 512, dtype=BF),
            arr(96, 512, dtype=BF),
            arr(512, 256, dtype=BF),
            arr(8, 256),
            arr(96, 256, dtype=BF),
            arr(TRACE_ROWS, 256),
        ],
        *mates,
        ranks,
        trace,
    )
    *wide, own_first, own_second = call(
        leave_kernel,
        [arr(48, 384), arr(48, 384), piece, piece],
        *moved, base, arrive_pick, send_kinds, trace, force_mine, force_other, select,
    )
    sent = [own_first, own_second]
    came = trade(*wide, acoustic)
    near, place, own_place, kinds, meet = call(
        faces_kernel,
        [
            arr(12, 256, 256, dtype=BF),
            arr(256, 512, dtype=BF),
            arr(256, 256, dtype=BF),
            arr(8, 256),
            arr(256, 256, dtype=BF),
        ],
        *mates,
        pick,
    )
    state, carry, force, base = call(
        first_inner_kernel,
        [whole, whole, arr(192, 512), arr(TRACE_ROWS, 256)],
        *moved, kept, arrive, force_mine, force_other, keep, near, interior, trace, lift_two,
        pick, send_kinds,
    )
    sending = [arr(12 * TRACE_ROWS, 256, dtype=BF), piece, piece]
    stacks, *later = call(
        first_outer_kernel,
        sending,
        *came, *sent, kinds, meet, reach_force, send_kinds, base, arrive_pick,
    )
    extra = [*came, arrive]
    for segment in range(1, 5):
        sent, came = later, trade(*later, acoustic)
        inner = functools.partial(inner_kernel, segment)
        args = [state, carry, force, stacks, place, near, interior, trace, lift_two]
        if segment == 4:
            (ahead,) = call(inner, [arr(256, 256)], *args)
            break
        outs = [whole, whole, arr(TRACE_ROWS, 256)]
        if segment == 1:
            state, carry, base, force = call(
                inner, [*outs, arr(192, 512)], *args, *extra, pick, send_kinds
            )
        else:
            state, carry, base = call(inner, outs, *args, pick, send_kinds)
        stacks, *later = call(
            functools.partial(outer_kernel, segment),
            sending,
            *came, *sent, kinds, meet, reach, send_kinds, base,
        )
    (out,) = call(
        last_kernel,
        [arr(256, 256)],
        *came, *sent, kinds, own_place, lift_two, ahead,
        far=True,
        scratch=(pltpu.VMEM((256, 256), F32), pltpu.SemaphoreType.DMA((2,))),
    )
    return out.reshape(4, 64, ELEMENTS)


def solution(mesh):
    in_specs = (
        P(None, None, ("sec", "dom")),
        P(("sec", "dom")),
        P(("sec", "dom")),
        P(("sec", "dom")),
        P(None, ("sec", "dom")),
    )
    out_specs = P(None, None, ("sec", "dom"))
    return jax.shard_map(step, mesh=mesh, in_specs=in_specs, out_specs=out_specs, check_vma=False)
```
